128 devices in a mesh: probe: 4 (over z_hi, core), sx: 4 (over x), sy: 8 (over y, z_lo).
Axes of the slice: x: 4, y: 4, z: 4 (z_hi: 2, z_lo: 2; z = z_hi * 2 + z_lo), core: 2. Of those that a mesh axis runs over, the one named last changes fastest.
Arguments:
- probes: float32 [8, 128, 256, 256], P('probe', 'sx', 'sy'), may hold values from -6 to 6
- velocity: float32 [3, 128, 256, 256], P(None, 'sx', 'sy'), may hold values from -0.15 to 0.15
- diffusivity: float32 [128, 256, 256], P('sx', 'sy'), may hold values from 0.02 to 0.15
- obs_weight: float32 [128, 256, 256], P('sx', 'sy'), may hold values from 0.05 to 1
Outputs:
- basis_fields: float32 [8, 128, 256, 256], P('probe', 'sx', 'sy')
- projected_hessian: float32 [8, 8], replicated
The draws below stay inside these ranges and needn't reach their ends.
All inputs are finite; a program needn't handle non-finite values.
Results may differ from the reference program's by a relative error of at most 0.00013.
Values sent between devices are 32-bit elements; how exact they have to be, the bound alone decides.
A program may use at most 128 MiB of HBM per device.

```python
import math
import jax
import jax.numpy as jnp
from jax import lax

CZ = 256
STEPS = 4
PROBES = 8
NX = 128
NY = 256
NCELLS = 8388608


def block_scale(rng, extent, pieces, least, high):
    level, own = 1.0, jax.random.fold_in(rng, 6)
    for axis_at, blocks in pieces:
        steps = jnp.exp(jax.random.uniform(jax.random.fold_in(own, axis_at), (blocks,), jnp.float32, least / len(pieces), high / len(pieces)))
        level = level * jnp.repeat(steps, extent[axis_at] // blocks).reshape([-1 if axis == axis_at else 1 for axis in range(len(extent))])
    return level


def normal_values(rng, dims, scale, most, split=(), held_as=jnp.bfloat16):
    values = jax.random.normal(rng, dims, jnp.float32) * scale
    if len(split) > 0:
        values = block_scale(rng, dims, split, -0.22, 0.18) * values
    return jnp.clip(values, min=-most, max=most).astype(held_as)


def setup_inputs(seed: int = 0) -> dict:
    key_list = jax.random.split(jax.random.key(seed), 5)
    probes = normal_values(key_list[0], (PROBES, NX, NY, CZ), 1.0, 6.0, ((0, 4), (1, 4), (2, 8)), jnp.float32)
    velocity = jnp.clip(jax.random.uniform(key_list[1], (3, NX, NY, CZ), jnp.float32, -0.15, 0.15) * block_scale(key_list[1], (3, NX, NY, CZ), ((1, 4), (2, 8)), -0.4, 0.0), -0.15, 0.15)
    diffusivity = jnp.clip(jnp.exp(math.log(0.15) - 2.014903 * jax.random.uniform(key_list[2], (NX, NY, CZ), jnp.float32) ** block_scale(key_list[2], (NX, NY, CZ), ((0, 4), (1, 8)), -0.2, 0.2)), 0.02, 0.15)
    obs_weight = jnp.clip(jnp.exp(math.log(1.0) - 2.9957323 * jax.random.uniform(key_list[3], (NX, NY, CZ), jnp.float32) ** block_scale(key_list[3], (NX, NY, CZ), ((0, 4), (1, 8)), -0.2, 0.2)), 0.05, 1.0)
    return {"probes": probes, "velocity": velocity, "diffusivity": diffusivity, "obs_weight": obs_weight}


def forward_step(state, coeffs):
    cc = coeffs[:, 1:-1, 1:-1, :]
    spread = cc[0]
    inner = state[:, 1:-1, 1:-1, :]
    padded = jnp.pad(inner, ((0, 0), (0, 0), (0, 0), (1, 1)))
    result = (1.0 - 6.0 * spread) * inner
    result = result + (spread - 0.5 * cc[1]) * state[:, 2:, 1:-1, :] + (spread + 0.5 * cc[1]) * state[:, :-2, 1:-1, :]
    result = result + (spread - 0.5 * cc[2]) * state[:, 1:-1, 2:, :] + (spread + 0.5 * cc[2]) * state[:, 1:-1, :-2, :]
    result = result + (spread - 0.5 * cc[3]) * padded[..., 2:] + (spread + 0.5 * cc[3]) * padded[..., :-2]
    return result

def adjoint_step(state, coeffs):
    spread = coeffs[0]
    plus_x = (spread - 0.5 * coeffs[1]) * state
    minus_x = (spread + 0.5 * coeffs[1]) * state
    plus_y = (spread - 0.5 * coeffs[2]) * state
    minus_y = (spread + 0.5 * coeffs[2]) * state
    cc = coeffs[:, 1:-1, 1:-1, :]
    inner = state[:, 1:-1, 1:-1, :]
    pad_plus = jnp.pad((cc[0] - 0.5 * cc[3]) * inner, ((0, 0), (0, 0), (0, 0), (1, 1)))
    pad_minus = jnp.pad((cc[0] + 0.5 * cc[3]) * inner, ((0, 0), (0, 0), (0, 0), (1, 1)))
    result = (1.0 - 6.0 * cc[0]) * inner
    result = result + plus_x[:, :-2, 1:-1, :] + minus_x[:, 2:, 1:-1, :]
    result = result + plus_y[:, 1:-1, :-2, :] + minus_y[:, 1:-1, 2:, :]
    result = result + pad_plus[..., :-2] + pad_minus[..., 2:]
    return result

def reference(probes, velocity, diffusivity, obs_weight):
    coeffs = jnp.concatenate([diffusivity[None], velocity], axis=0)
    coeffs = jnp.pad(coeffs, ((0, 0), (1, 1), (1, 1), (0, 0)))
    widths = ((0, 0), (1, 1), (1, 1), (0, 0))

    def hessian(field):
        state = field[None]
        for step in range(STEPS):
            state = forward_step(jnp.pad(state, widths), coeffs)
        state = obs_weight * state
        for step in range(STEPS):
            state = adjoint_step(jnp.pad(state, widths), coeffs)
        return state[0]
    images = lax.map(hessian, probes)
    flat = images.reshape(PROBES, -1)
    gram = jnp.dot(flat, flat.T, precision=lax.Precision.HIGHEST) / NCELLS
    lower = jnp.linalg.cholesky(gram)
    inverse = jax.scipy.linalg.solve_triangular(lower, jnp.eye(PROBES, dtype=jnp.float32), lower=True)
    basis = jnp.dot(inverse, flat, precision=lax.Precision.HIGHEST)
    basis_fields = basis.reshape(images.shape)
    second = lax.map(hessian, basis_fields).reshape(PROBES, -1)
    projected = jnp.dot(basis, second.T, precision=lax.Precision.HIGHEST) / NCELLS
    return (basis_fields, projected)
```

```python
import jax
import jax.numpy as jnp
from jax import lax
from jax.sharding import PartitionSpec as P

STEPS = 4


def extended(value, sides, width):
    for axis, dim in sides:
        devices, length = (lax.axis_size(axis), value.shape[dim])
        up = [(i, (i + 1) % devices) for i in range(devices - 1)]
        down = [(j, i) for i, j in up]
        last = lax.slice_in_dim(value, length - width, length, axis=dim)
        leading = lax.slice_in_dim(value, 0, width, axis=dim)
        before = lax.ppermute(last, axis, up)
        after = lax.ppermute(leading, axis, down)
        value = jnp.concatenate([before, value, after], axis=dim)
    return value


def forward_step(state, coeffs):
    cc = coeffs[:, 1:-1, 1:-1, :]
    spread = cc[0]
    inner = state[:, 1:-1, 1:-1, :]
    padded = jnp.pad(inner, ((0, 0), (0, 0), (0, 0), (1, 1)))
    result = (1.0 - 6.0 * spread) * inner
    result = (
        result
        + (spread - 0.5 * cc[1]) * state[:, 2:, 1:-1, :]
        + (spread + 0.5 * cc[1]) * state[:, :-2, 1:-1, :]
    )
    result = (
        result
        + (spread - 0.5 * cc[2]) * state[:, 1:-1, 2:, :]
        + (spread + 0.5 * cc[2]) * state[:, 1:-1, :-2, :]
    )
    result = (
        result
        + (spread - 0.5 * cc[3]) * padded[..., 2:]
        + (spread + 0.5 * cc[3]) * padded[..., :-2]
    )
    return result


def adjoint_step(state, coeffs):
    spread = coeffs[0]
    plus_x = (spread - 0.5 * coeffs[1]) * state
    minus_x = (spread + 0.5 * coeffs[1]) * state
    plus_y = (spread - 0.5 * coeffs[2]) * state
    minus_y = (spread + 0.5 * coeffs[2]) * state
    cc = coeffs[:, 1:-1, 1:-1, :]
    inner = state[:, 1:-1, 1:-1, :]
    pad_plus = jnp.pad((cc[0] - 0.5 * cc[3]) * inner, ((0, 0), (0, 0), (0, 0), (1, 1)))
    pad_minus = jnp.pad((cc[0] + 0.5 * cc[3]) * inner, ((0, 0), (0, 0), (0, 0), (1, 1)))
    result = (1.0 - 6.0 * cc[0]) * inner
    result = result + plus_x[:, :-2, 1:-1, :] + minus_x[:, 2:, 1:-1, :]
    result = result + plus_y[:, 1:-1, :-2, :] + minus_y[:, 1:-1, 2:, :]
    result = result + pad_plus[..., :-2] + pad_minus[..., 2:]
    return result


def factor_inverse(gram, count):
    lower = jnp.linalg.cholesky(gram)
    return jax.scipy.linalg.solve_triangular(lower, jnp.eye(count, dtype=jnp.float32), lower=True)


def shards(probes, velocity, diffusivity, obs_weight):
    group = probes.shape[0]
    count = group * lax.axis_size("probe")
    ncells = (
        probes.shape[1]
        * probes.shape[2]
        * probes.shape[3]
        * lax.axis_size("sx")
        * lax.axis_size("sy")
    )
    coeffs = jnp.concatenate([diffusivity[None], velocity], axis=0)
    highest = lax.Precision.HIGHEST
    edge_coeffs = extended(coeffs, (("sx", 1), ("sy", 2)), 1)

    def forward(state):
        for step in range(STEPS):
            padded = extended(state, (("sx", 1), ("sy", 2)), 1)
            state = forward_step(padded, edge_coeffs)
        return state

    state = obs_weight * forward(probes)
    for step in range(STEPS):
        padded = extended(state, (("sx", 1), ("sy", 2)), 1)
        state = adjoint_step(padded, edge_coeffs)
    images = state
    again = forward(images)
    root = jnp.sqrt(obs_weight) * again
    both = jnp.stack([images, root], axis=1)
    slabs = lax.all_to_all(both, "probe", split_axis=2, concat_axis=0, tiled=True)
    flat = slabs[:, 0].reshape(count, -1)
    flat_root = slabs[:, 1].reshape(count, -1)
    partial_gram = jnp.dot(flat, flat.T, precision=highest)
    partial_cross = jnp.dot(flat_root, flat_root.T, precision=highest)
    sums = lax.psum(jnp.stack([partial_gram, partial_cross]), ("probe", "sx", "sy")) / ncells
    gram, cross = sums[0], sums[1]
    inverse = factor_inverse(gram, count)
    basis_slab = jnp.dot(inverse, flat, precision=highest)
    basis_fields = lax.all_to_all(
        basis_slab.reshape(slabs[:, 0].shape), "probe", split_axis=0, concat_axis=1, tiled=True
    )
    projected = jnp.dot(
        jnp.dot(inverse, cross, precision=highest), inverse.T, precision=highest
    )
    return (basis_fields, projected)


def solution(mesh):
    return jax.shard_map(
        shards,
        mesh=mesh,
        in_specs=(
            P("probe", "sx", "sy", None),
            P(None, "sx", "sy", None),
            P("sx", "sy", None),
            P("sx", "sy", None),
        ),
        out_specs=(P("probe", "sx", "sy", None), P()),
        check_vma=False,
    )
```

```python
import functools

import jax
import jax.numpy as jnp
from jax import lax
from jax.experimental import pallas as pl
from jax.experimental.pallas import tpu as pltpu
from jax.sharding import PartitionSpec as P

STEPS = 4
MESH = pl.DeviceIdType.MESH
LANES = 128
C0, PX, MX, PY, MY, PZ, MZ = range(7)


def spread(value, shape):
    return jnp.broadcast_to(value, shape)


def kernel(
    cells,
    probes,
    velocity,
    diffusivity,
    weight,
    basis,
    projected,
    state,
    coef,
    edge_tile,
    edge_row,
    images,
    x_out,
    x_in,
    y_out,
    y_in,
    sums_probe,
    sums_sx,
    sums_sy,
    inverse_ref,
    x_send,
    x_recv,
    y_send,
    y_recv,
    image_send,
    image_recv,
    sum_send,
    sum_recv,
):
    group, nx, ny, nz = probes.shape
    at = {name: lax.axis_index(name) for name in ("probe", "sx", "sy")}
    size = {name: lax.axis_size(name) for name in ("probe", "sx", "sy")}
    me = at["probe"]

    barrier = pltpu.get_barrier_semaphore()
    peers = 0
    for name in ("probe", "sx", "sy"):
        for shift in range(1, size[name]):
            peer = lax.rem(at[name] + shift, size[name])
            pl.semaphore_signal(barrier, inc=1, device_id={name: peer}, device_id_type=MESH)
            peers += 1

    rows = lax.broadcasted_iota(jnp.int32, (ny, nz), 0)
    cols = lax.broadcasted_iota(jnp.int32, (ny, nz), 1)
    tile_rows = lax.broadcasted_iota(jnp.int32, (8, nz), 0)
    zero = jnp.zeros((ny, nz), jnp.float32)

    def prepare(x, carry):
        k = diffusivity[x]
        hx, hy, hz = (0.5 * velocity[d, x] for d in range(3))
        coef[C0, x + 1] = 1.0 - 6.0 * k
        coef[PX, x + 1] = k - hx
        coef[MX, x + 1] = k + hx
        plus, minus = k - hy, k + hy
        coef[PY, x + 1] = jnp.where(rows == ny - 1, 0.0, plus)
        coef[MY, x + 1] = jnp.where(rows == 0, 0.0, minus)
        edge_tile[0, x] = jnp.where(tile_rows == 0, minus[0:8], 0.0)
        edge_tile[1, x] = jnp.where(tile_rows == 7, plus[ny - 8 : ny], 0.0)
        edge_row[0, x] = minus[0:1]
        edge_row[1, x] = plus[ny - 1 : ny]
        coef[PZ, x + 1] = jnp.where(cols == nz - 1, 0.0, k - hz)
        coef[MZ, x + 1] = jnp.where(cols == 0, 0.0, k + hz)
        for p in range(group):
            state[0, p, x + 1] = probes[p, x]
        return carry

    lax.fori_loop(0, nx, prepare, 0)
    for x in (0, nx + 1):
        coef[PX, x] = zero
        coef[MX, x] = zero
        for slot in range(2):
            for p in range(group):
                state[slot, p, x] = zero

    pl.semaphore_wait(barrier, peers)

    has = {}
    for name in ("sx", "sy"):
        has[name] = (at[name] > 0, at[name] < size[name] - 1)

    def face(name, side, slot):
        out, into = (x_out, x_in) if name == "sx" else (y_out, y_in)
        send, recv = (x_send, x_recv) if name == "sx" else (y_send, y_recv)
        step = 1 if side else -1
        return pltpu.make_async_remote_copy(
            src_ref=out.at[side],
            dst_ref=into.at[slot, 1 - side],
            send_sem=send.at[side],
            recv_sem=recv.at[slot, 1 - side],
            device_id={name: at[name] + step},
            device_id_type=MESH,
        )

    def arriving(name, side, slot):
        into = x_in if name == "sx" else y_in
        out = x_out if name == "sx" else y_out
        send, recv = (x_send, x_recv) if name == "sx" else (y_send, y_recv)
        step = 1 if side else -1
        return pltpu.make_async_remote_copy(
            src_ref=out.at[side],
            dst_ref=into.at[slot, side],
            send_sem=send.at[side],
            recv_sem=recv.at[slot, side],
            device_id={name: at[name] + step},
            device_id_type=MESH,
        )

    def fill(now, adjoint):
        def one(x, carry):
            for p in range(group):
                low = state[now, p, x + 1, 0:1, :]
                high = state[now, p, x + 1, ny - 1 : ny, :]
                if adjoint:
                    low = low * edge_row[0, x]
                    high = high * edge_row[1, x]
                y_out[0, p, x] = low
                y_out[1, p, x] = high
            return carry

        lax.fori_loop(0, nx, one, 0)
        for p in range(group):
            low, high = state[now, p, 1], state[now, p, nx]
            if adjoint:
                low, high = low * coef[MX, 1], high * coef[PX, nx]
            x_out[0, p] = low
            x_out[1, p] = high

    def local(now, later, adjoint):
        def plane(x, carry):
            for p in range(group):
                u = state[now, p, x]
                before, after = state[now, p, x - 1], state[now, p, x + 1]
                if adjoint:
                    r = coef[C0, x] * u
                    r = r + coef[PX, x - 1] * before + coef[MX, x + 1] * after
                    r = r + pltpu.roll(coef[PY, x] * u, 1, 0)
                    r = r + pltpu.roll(coef[MY, x] * u, ny - 1, 0)
                    r = r + pltpu.roll(coef[PZ, x] * u, 1, 1)
                    r = r + pltpu.roll(coef[MZ, x] * u, nz - 1, 1)
                else:
                    r = coef[C0, x] * u
                    r = r + coef[PX, x] * after + coef[MX, x] * before
                    r = r + coef[PY, x] * pltpu.roll(u, ny - 1, 0)
                    r = r + coef[MY, x] * pltpu.roll(u, 1, 0)
                    r = r + coef[PZ, x] * pltpu.roll(u, nz - 1, 1)
                    r = r + coef[MZ, x] * pltpu.roll(u, 1, 1)
                state[later, p, x] = r
            return carry

        lax.fori_loop(1, nx + 1, plane, 0)

    def fix_x(later, slot, side, adjoint):
        x = nx if side else 1
        for p in range(group):
            got = x_in[slot, side, p]
            if not adjoint:
                got = got * coef[PX if side else MX, x]
            state[later, p, x] = state[later, p, x] + got

    def fix_y(later, slot, side, adjoint):
        first = ny - 8 if side else 0

        def one(x, carry):
            for p in range(group):
                got = spread(y_in[slot, side, p, x], (8, nz))
                if adjoint:
                    got = jnp.where(tile_rows == (7 if side else 0), got, 0.0)
                else:
                    got = got * edge_tile[side, x]
                tile = state[later, p, x + 1, first : first + 8, :]
                state[later, p, x + 1, first : first + 8, :] = tile + got
            return carry

        lax.fori_loop(0, nx, one, 0)

    def steps(adjoint):
        def step(i, carry):
            now = lax.rem(i, 2)
            later = 1 - now
            fill(now, adjoint)
            for name in ("sy", "sx"):
                for side in range(2):

                    @pl.when(has[name][side])
                    def _():
                        face(name, side, now).start()

            local(now, later, adjoint)
            for name in ("sx", "sy"):
                for side in range(2):

                    @pl.when(has[name][side])
                    def _():
                        face(name, side, now).wait_send()
                        arriving(name, side, now).wait_recv()
                        if name == "sx":
                            fix_x(later, now, side, adjoint)
                        else:
                            fix_y(later, now, side, adjoint)

            return carry

        lax.fori_loop(0, STEPS, step, 0)

    def apply():
        steps(False)

        def scale(x, carry):
            for p in range(group):
                state[0, p, x + 1] = state[0, p, x + 1] * weight[x]
            return carry

        lax.fori_loop(0, nx, scale, 0)
        steps(True)

    def image_copy(pair, target, sem):
        return pltpu.make_async_remote_copy(
            src_ref=images.at[pl.ds(group * pair, group)],
            dst_ref=images.at[pl.ds(group * pair, group)],
            send_sem=image_send.at[sem],
            recv_sem=image_recv.at[pair],
            device_id={"probe": target},
            device_id_type=MESH,
        )

    apply()

    def keep(x, carry):
        for p in range(group):
            images[group * me + p, x] = state[0, p, x + 1]
        return carry

    lax.fori_loop(0, nx, keep, 0)

    @pl.when(me == 0)
    def _():
        image_copy(0, 2, 1).start()
        image_copy(0, 1, 0).start()

    @pl.when(me == 1)
    def _():
        image_copy(1, 3, 0).start()

    @pl.when(me == 2)
    def _():
        image_copy(2, 3, 0).start()

    apply()

    @pl.when(me == 0)
    def _():
        image_copy(0, 2, 1).wait_send()
        image_copy(0, 1, 0).wait_send()

    @pl.when(me == 1)
    def _():
        image_copy(1, 3, 0).wait_send()
        image_copy(0, 2, 1).wait_recv()

    @pl.when(me == 2)
    def _():
        image_copy(0, 3, 1).wait_recv()
        image_copy(0, 3, 1).start()
        image_copy(1, 3, 1).wait_recv()
        image_copy(2, 3, 0).wait_send()
        image_copy(0, 3, 1).wait_send()

    @pl.when(me == 3)
    def _():
        image_copy(1, 2, 0).wait_recv()
        image_copy(1, 2, 0).start()
        image_copy(2, 2, 0).wait_recv()
        image_copy(0, 2, 0).wait_recv()
        image_copy(1, 2, 0).wait_send()

    trow = lax.broadcasted_iota(jnp.int32, (8, LANES), 0)
    tcol = lax.broadcasted_iota(jnp.int32, (8, LANES), 1)
    count = size["probe"] * group

    def inner(k, total):
        def plane(x, acc):
            own = [images[group * me + j, x] for j in range(group)]
            second = [state[0, j, x + 1] for j in range(group)]
            acc = list(acc)
            for i in range(group):
                other = images[group * k + i, x]
                for j in range(group):
                    for m, right in enumerate((own[j], second[j])):
                        n = (i * group + j) * 2 + m
                        prod = other * right
                        for y in range(0, ny, 8):
                            acc[n] = acc[n] + prod[y : y + 8]
            return tuple(acc)

        start = tuple(jnp.zeros((8, nz), jnp.float32) for _ in range(group * group * 2))
        acc = lax.fori_loop(0, nx, plane, start)
        for i in range(group):
            for j in range(group):
                for m in range(2):
                    value = jnp.sum(acc[(i * group + j) * 2 + m])
                    low, high = group * k + i, group * me + j
                    here = jnp.logical_and(trow == low, tcol == high + count * m)
                    there = jnp.logical_and(trow == high, tcol == low + count * m)
                    there = jnp.logical_and(there, k < me)
                    total = jnp.where(jnp.logical_or(here, there), value, total)
        return total

    total = lax.fori_loop(0, me + 1, inner, jnp.zeros((8, LANES), jnp.float32))

    sem = 0
    for name, sums in (("probe", sums_probe), ("sx", sums_sx), ("sy", sums_sy)):
        mine = at[name]
        sums[mine] = total

        def part(shift, sem):
            return pltpu.make_async_remote_copy(
                src_ref=sums.at[mine],
                dst_ref=sums.at[mine],
                send_sem=sum_send.at[sem],
                recv_sem=sum_recv.at[sem],
                device_id={name: lax.rem(mine + shift, size[name])},
                device_id_type=MESH,
            )

        for shift in range(1, size[name]):
            part(shift, sem + shift - 1).start()
        for shift in range(1, size[name]):
            part(shift, sem + shift - 1).wait()
        sem += size[name] - 1
        total = sums[0]
        for other in range(1, size[name]):
            total = total + sums[other]

    full = (8, LANES)
    work = total / cells
    work = jnp.where(tcol == trow + 2 * count, 1.0, work)
    for j in range(count):
        pivot_row = spread(work[j : j + 1, :], full)
        column = spread(work[:, j : j + 1], full)
        pivot = spread(work[j : j + 1, j : j + 1], full)
        work = work - jnp.where(trow > j, column / pivot, 0.0) * pivot_row
    diagonal = jnp.sum(jnp.where(trow == tcol, work, 0.0), axis=1, keepdims=True)
    work = work / spread(jnp.sqrt(diagonal), full)
    inverse = jnp.where(tcol < count, pltpu.roll(work, LANES - 2 * count, 1), 0.0)
    half = jnp.where(tcol < count, pltpu.roll(work, LANES - count, 1), 0.0)
    product = lax.dot_general(
        half,
        inverse,
        (((1,), (1,)), ((), ())),
        precision=lax.Precision.HIGHEST,
        preferred_element_type=jnp.float32,
    )
    projected[...] = product
    inverse_ref[...] = inverse

    for g in range(size["probe"]):

        @pl.when(me == g)
        def _():
            inv = inverse_ref[...]
            factor = [
                [
                    jnp.sum(jnp.where((trow == group * g + r) & (tcol == i), inv, 0.0))
                    for i in range(group * g + r + 1)
                ]
                for r in range(group)
            ]

            def plane(x, carry):
                field = [images[i, x] for i in range(group * (g + 1))]
                for r in range(group):
                    out = factor[r][0] * field[0]
                    for i in range(1, group * g + r + 1):
                        out = out + factor[r][i] * field[i]
                    basis[r, x] = out
                return carry

            lax.fori_loop(0, nx, plane, 0)


def shards(probes, velocity, diffusivity, obs_weight):
    group, nx, ny, nz = probes.shape
    nprobe, nsx, nsy = (lax.axis_size(name) for name in ("probe", "sx", "sy"))
    count = group * nprobe
    cells = float(nx * nsx * ny * nsy * nz)
    vmem = pl.BlockSpec(memory_space=pltpu.VMEM)
    f32 = jnp.float32
    total = nprobe + nsx + nsy - 3
    return pl.pallas_call(
        functools.partial(kernel, cells),
        out_shape=(
            jax.ShapeDtypeStruct(probes.shape, f32),
            jax.ShapeDtypeStruct((count, count), f32),
        ),
        in_specs=[vmem] * 4,
        out_specs=(vmem, vmem),
        scratch_shapes=[
            pltpu.VMEM((2, group, nx + 2, ny, nz), f32),
            pltpu.VMEM((7, nx + 2, ny, nz), f32),
            pltpu.VMEM((2, nx, 8, nz), f32),
            pltpu.VMEM((2, nx, 1, nz), f32),
            pltpu.VMEM((count, nx, ny, nz), f32),
            pltpu.VMEM((2, group, ny, nz), f32),
            pltpu.VMEM((2, 2, group, ny, nz), f32),
            pltpu.VMEM((2, group, nx, 1, nz), f32),
            pltpu.VMEM((2, 2, group, nx, 1, nz), f32),
            pltpu.VMEM((nprobe, 8, LANES), f32),
            pltpu.VMEM((nsx, 8, LANES), f32),
            pltpu.VMEM((nsy, 8, LANES), f32),
            pltpu.VMEM((8, LANES), f32),
            pltpu.SemaphoreType.DMA((2,)),
            pltpu.SemaphoreType.DMA((2, 2)),
            pltpu.SemaphoreType.DMA((2,)),
            pltpu.SemaphoreType.DMA((2, 2)),
            pltpu.SemaphoreType.DMA((2,)),
            pltpu.SemaphoreType.DMA((nprobe,)),
            pltpu.SemaphoreType.DMA((total,)),
            pltpu.SemaphoreType.DMA((total,)),
        ],
        compiler_params=pltpu.CompilerParams(
            collective_id=0, has_side_effects=True, vmem_limit_bytes=60 * 1024 * 1024
        ),
    )(probes, velocity, diffusivity, obs_weight)


def solution(mesh):
    return jax.shard_map(
        shards,
        mesh=mesh,
        in_specs=(
            P("probe", "sx", "sy", None),
            P(None, "sx", "sy", None),
            P("sx", "sy", None),
            P("sx", "sy", None),
        ),
        out_specs=(P("probe", "sx", "sy", None), P()),
        check_vma=False,
    )
```

```python
import functools

import jax
import jax.numpy as jnp
from jax import lax
from jax.experimental import pallas as pl
from jax.experimental.pallas import tpu as pltpu
from jax.sharding import PartitionSpec as P

STEPS = 4
UNROLL = 1
MESH = pl.DeviceIdType.MESH
LANES = 128
C0, PX, MX, PY, MY, PZ, MZ = range(7)


def spread(value, shape):
    return jnp.broadcast_to(value, shape)


def kernel(
    cells,
    probes,
    velocity,
    diffusivity,
    weight,
    basis,
    projected,
    field,
    other_field,
    center,
    coef,
    edge,
    got_probes,
    got_velocity,
    got_diffusivity,
    got_weight,
    images,
    x_in,
    y_out,
    y_in,
    sums_probe,
    sums_sx,
    sums_sy,
    inverse_ref,
    x_send,
    x_recv,
    y_send,
    y_recv,
    edge_send,
    edge_recv,
    image_send,
    image_recv,
    sum_send,
    sum_recv,
    in_sem,
    out_sem,
):
    group, nx, ny, nz = probes.shape
    deep, wide = ny // 8, nz // LANES
    at = {name: lax.axis_index(name) for name in ("probe", "sx", "sy")}
    size = {name: lax.axis_size(name) for name in ("probe", "sx", "sy")}
    me = at["probe"]
    has = {name: (at[name] > 0, at[name] < size[name] - 1) for name in ("sx", "sy")}

    def tile(t):
        return slice(t * LANES, (t + 1) * LANES)

    parts = 4 if nx % 4 == 0 else 1
    per = nx // parts

    def moved(ref, lead, part, t):
        return ref.at[lead + (pl.ds(part * per, per), slice(None), pl.ds(t * LANES, LANES))]

    def held(ref, lead, part, t):
        return ref.at[lead + (pl.ds(part * per, per), t)]

    arriving = {}
    for part in range(parts):
        for n, (src, dst, lead) in enumerate(
            (
                (diffusivity, got_diffusivity, ()),
                (velocity, got_velocity, (slice(None),)),
                (probes, got_probes, (slice(None),)),
                (weight, got_weight, ()),
            )
        ):
            for t in range(wide):
                copy = pltpu.make_async_copy(
                    moved(src, lead, part, t), held(dst, lead, part, t), in_sem.at[part, n, t]
                )
                arriving[part, n, t] = copy
                copy.start()

    def rows_of(ref, index, l, t):
        return ref[index + (t, pl.ds(l, 8, stride=deep), slice(None))]

    srow = lax.broadcasted_iota(jnp.int32, (8, LANES), 0)
    lane = lax.broadcasted_iota(jnp.int32, (8, LANES), 1)
    zero = jnp.zeros((8, LANES), jnp.float32)

    def shift_z(tiles, up):
        rolled = [pltpu.roll(v, LANES - 1 if up else 1, 1) for v in tiles]
        out = []
        for t in range(wide):
            other = t + 1 if up else t - 1
            if 0 <= other < wide:
                out.append(jnp.where(lane == (LANES - 1 if up else 0), rolled[other], rolled[t]))
            else:
                out.append(rolled[t])
        return out

    def shift_y(tiles, l, up):
        if up:
            return tiles[l + 1] if l + 1 < deep else pltpu.roll(tiles[0], 7, 0)
        return tiles[l - 1] if l > 0 else pltpu.roll(tiles[deep - 1], 1, 0)

    for x in (0, nx + 1):
        for l in range(deep):
            for t in range(wide):
                for ref in (field, other_field):
                    for p in range(group):
                        ref[p, x, l, :, tile(t)] = zero
    for l in range(deep):
        for t in range(wide):
            coef[1, MX, 1, l, :, tile(t)] = zero
            coef[1, PX, nx, l, :, tile(t)] = zero

    barrier = pltpu.get_barrier_semaphore()
    peers = 0
    for name in ("probe", "sx", "sy"):
        for shift in range(1, size[name]):
            peer = lax.rem(at[name] + shift, size[name])
            pl.semaphore_signal(barrier, inc=1, device_id={name: peer}, device_id_type=MESH)
            peers += 1

    def prepare(x, carry):
        last, first = nz - LANES, 0
        plus_y, minus_y = [], []
        for t in range(wide):
            plus_y.append([])
            minus_y.append([])
            for l in range(deep):
                k = rows_of(got_diffusivity, (x,), l, t)
                hx, hy = (0.5 * rows_of(got_velocity, (d, x), l, t) for d in range(2))
                center[x + 1, l, :, tile(t)] = 1.0 - 6.0 * k
                coef[0, PX, x + 1, l, :, tile(t)] = k - hx
                coef[0, MX, x + 1, l, :, tile(t)] = k + hx
                coef[1, MX, x + 2, l, :, tile(t)] = k - hx
                coef[1, PX, x, l, :, tile(t)] = k + hx
                plus_y[t].append(k - hy)
                minus_y[t].append(k + hy)
                for p in range(group):
                    field[p, x + 1, l, :, tile(t)] = rows_of(got_probes, (p, x), l, t)
            edge[0, 0, x, :, tile(t)] = minus_y[t][0][0:1]
            edge[0, 1, x, :, tile(t)] = plus_y[t][deep - 1][7:8]
            for l in range(deep):
                up, down = shift_y(minus_y[t], l, True), shift_y(plus_y[t], l, False)
                plus, minus = plus_y[t][l], minus_y[t][l]
                if l == deep - 1:
                    up, plus = (jnp.where(srow == 7, 0.0, v) for v in (up, plus))
                if l == 0:
                    down, minus = (jnp.where(srow == 0, 0.0, v) for v in (down, minus))
                coef[0, PY, x + 1, l, :, tile(t)] = plus
                coef[0, MY, x + 1, l, :, tile(t)] = minus
                coef[1, PY, x + 1, l, :, tile(t)] = up
                coef[1, MY, x + 1, l, :, tile(t)] = down
        for l in range(deep):
            ks = [rows_of(got_diffusivity, (x,), l, t) for t in range(wide)]
            hs = [0.5 * rows_of(got_velocity, (2, x), l, t) for t in range(wide)]
            plus = [k - h for k, h in zip(ks, hs)]
            minus = [k + h for k, h in zip(ks, hs)]
            up, down = shift_z(minus, True), shift_z(plus, False)
            for v in (plus, up):
                v[wide - 1] = jnp.where(lane == LANES - 1, 0.0, v[wide - 1])
            for v in (minus, down):
                v[0] = jnp.where(lane == 0, 0.0, v[0])
            for t in range(wide):
                coef[0, PZ, x + 1, l, :, tile(t)] = plus[t]
                coef[0, MZ, x + 1, l, :, tile(t)] = minus[t]
                coef[1, PZ, x + 1, l, :, tile(t)] = up[t]
                coef[1, MZ, x + 1, l, :, tile(t)] = down[t]
        return carry

    for part in range(parts):
        for n in range(3):
            for t in range(wide):
                arriving[part, n, t].wait()
        lax.fori_loop(part * per, (part + 1) * per, prepare, 0)

    def fill():
        def one(x, carry):
            for p in range(group):
                for t in range(wide):
                    y_out[0, p, x, :, tile(t)] = field[p, x + 1, 0, 0:1, tile(t)]
                    y_out[1, p, x, :, tile(t)] = field[p, x + 1, deep - 1, 7:8, tile(t)]
            return carry

        lax.fori_loop(0, nx, one, 0)

    fill()
    pl.semaphore_wait(barrier, peers)

    def remote(src, dst, send, recv, name, target):
        return pltpu.make_async_remote_copy(
            src_ref=src,
            dst_ref=dst,
            send_sem=send,
            recv_sem=recv,
            device_id={name: target},
            device_id_type=MESH,
        )

    def edges(name, side, came):
        n = 0 if name == "sx" else 1
        into = side if came else 1 - side
        if name == "sx":
            src = coef.at[0, PX, nx] if side else coef.at[0, MX, 1]
            dst = coef.at[1, PX, nx] if into else coef.at[1, MX, 1]
        else:
            src, dst = edge.at[0, side], edge.at[1, into]
        target = at[name] + (1 if side else -1)
        return remote(src, dst, edge_send.at[n, side], edge_recv.at[n, into], name, target)

    def face(name, side, now, came=False):
        into = side if came else 1 - side
        target = at[name] + (1 if side else -1)
        if name == "sx":
            ref = other_field if now else field
            src, dst = ref.at[:, nx if side else 1], x_in.at[now, into]
            return remote(src, dst, x_send.at[side], x_recv.at[now, into], name, target)
        src, dst = y_out.at[side], y_in.at[now, into]
        return remote(src, dst, y_send.at[side], y_recv.at[now, into], name, target)

    def local(old, new, mode):
        def plane(x, carry):
            for p in range(group):
                u = [[old[p, x, l, :, tile(t)] for t in range(wide)] for l in range(deep)]
                by_tile = [[u[l][t] for l in range(deep)] for t in range(wide)]
                for l in range(deep):
                    up_z, down_z = shift_z(u[l], True), shift_z(u[l], False)
                    for t in range(wide):
                        w = tile(t)
                        r = center[x, l, :, w] * u[l][t]
                        r = r + (
                            coef[mode, PX, x, l, :, w] * old[p, x + 1, l, :, w]
                            + coef[mode, MX, x, l, :, w] * old[p, x - 1, l, :, w]
                        )
                        r = r + (
                            coef[mode, PY, x, l, :, w] * shift_y(by_tile[t], l, True)
                            + coef[mode, MY, x, l, :, w] * shift_y(by_tile[t], l, False)
                        )
                        r = r + (
                            coef[mode, PZ, x, l, :, w] * up_z[t]
                            + coef[mode, MZ, x, l, :, w] * down_z[t]
                        )
                        new[p, x, l, :, w] = r
            return carry

        lax.fori_loop(1, nx + 1, plane, 0, unroll=UNROLL)

    def fix_x(slot, new, side, mode):
        x = nx if side else 1
        for l in range(deep):
            for t in range(wide):
                w = tile(t)
                c = coef[mode, PX if side else MX, x, l, :, w]
                for p in range(group):
                    add = c * x_in[slot, side, p, l, :, w]
                    new[p, x, l, :, w] = new[p, x, l, :, w] + add

    def fix_y(slot, new, side, mode):
        l, row = (deep - 1, 7) if side else (0, 0)

        def one(x, carry):
            for t in range(wide):
                w = tile(t)
                c = spread(edge[mode, side, x, :, w], (8, LANES))
                for p in range(group):
                    add = c * spread(y_in[slot, side, p, x, :, w], (8, LANES))
                    v = new[p, x + 1, l, :, w] + jnp.where(srow == row, add, 0.0)
                    new[p, x + 1, l, :, w] = v
                    y_out[side, p, x, :, w] = v[row : row + 1]
            return carry

        lax.fori_loop(0, nx, one, 0, unroll=4)

    chunks = 2 * STEPS
    thick = nx // chunks if nx >= chunks else nx

    def image_copy(pair, target, sem, chunk=None):
        lead = pl.ds(group * pair, group)
        if chunk is None:
            ref, recv, send = images.at[lead], image_recv.at[pair, 0], image_send.at[sem, 0]
        else:
            ref = images.at[lead, pl.ds(chunk * thick, thick)]
            recv, send = image_recv.at[pair, chunk], image_send.at[sem, chunk]
        return remote(ref, ref, send, recv, "probe", target)

    def relay(chunk):
        @pl.when(me == 2)
        def _():
            image_copy(0, 3, 1, chunk).wait_recv()
            image_copy(0, 3, 1, chunk).start()

        @pl.when(me == 3)
        def _():
            image_copy(1, 2, 1, chunk).wait_recv()
            image_copy(1, 2, 1, chunk).start()

    def run(second):
        def step(i, now, mode):
            old, new = (other_field, field) if now else (field, other_field)
            for name in ("sy", "sx"):
                for side in range(2):

                    @pl.when(has[name][side])
                    def _():
                        face(name, side, now).start()

            if second:

                @pl.when(me < 2)
                def _():
                    image_copy(me, me + 2, 1, i).start()

            local(old, new, mode)
            if second:

                @pl.when(i >= 2)
                def _():
                    relay(i - 2)

            for name in ("sx", "sy"):
                for side in range(2):

                    @pl.when(has[name][side])
                    def _():
                        face(name, side, now).wait_send()
                        face(name, side, now, True).wait_recv()
                        (fix_x if name == "sx" else fix_y)(now, new, side, mode)

        def both(i, carry):
            mode = 2 * i // STEPS
            step(2 * i, 0, mode)
            step(2 * i + 1, 1, mode)

            @pl.when(2 * i == STEPS - 2)
            def _():
                def weigh(x, carry):
                    for l in range(deep):
                        for t in range(wide):
                            w = tile(t)
                            c = rows_of(got_weight, (x,), l, t)
                            for p in range(group):
                                v = c * field[p, x + 1, l, :, w]
                                field[p, x + 1, l, :, w] = v
                                if l == 0:
                                    y_out[0, p, x, :, w] = v[0:1]
                                if l == deep - 1:
                                    y_out[1, p, x, :, w] = v[7:8]
                    return carry

                lax.fori_loop(0, nx, weigh, 0)
                if not second:
                    for name in ("sx", "sy"):
                        for side in range(2):

                            @pl.when(has[name][side])
                            def _():
                                edges(name, side, False).wait_send()
                                edges(name, side, True).wait_recv()

            return carry

        lax.fori_loop(0, STEPS, both, 0)

    for name in ("sx", "sy"):
        for side in range(2):

            @pl.when(has[name][side])
            def _():
                edges(name, side, False).start()

    for part in range(parts):
        for t in range(wide):
            arriving[part, 3, t].wait()

    run(False)

    def keep(x, carry):
        for p in range(group):
            images[group * me + p, x] = field[p, x + 1]
        return carry

    lax.fori_loop(0, nx, keep, 0)


    @pl.when(me == 0)
    def _():
        image_copy(0, 1, 0).start()

    @pl.when(me == 2)
    def _():
        image_copy(2, 3, 0).start()

    run(True)

    for chunk in range(chunks - 2, chunks):
        relay(chunk)

    @pl.when(me == 0)
    def _():
        image_copy(0, 1, 0).wait_send()
        for chunk in range(chunks):
            image_copy(0, 2, 1, chunk).wait_send()

    @pl.when(me == 1)
    def _():
        image_copy(0, 2, 1).wait_recv()
        for chunk in range(chunks):
            image_copy(1, 3, 1, chunk).wait_send()

    @pl.when(me == 2)
    def _():
        image_copy(2, 3, 0).wait_send()
        for chunk in range(chunks):
            image_copy(0, 3, 1, chunk).wait_send()
            image_copy(1, 3, 1, chunk).wait_recv()

    @pl.when(me == 3)
    def _():
        image_copy(2, 2, 0).wait_recv()
        for chunk in range(chunks):
            image_copy(1, 2, 1, chunk).wait_send()
            image_copy(0, 2, 1, chunk).wait_recv()

    trow, tcol = srow, lane
    count = size["probe"] * group

    def inner(k, total):
        def plane(x, acc):
            acc = list(acc)
            for l in range(deep):
                own = [images[group * me + j, x, l] for j in range(group)]
                second = [field[j, x + 1, l] for j in range(group)]
                for i in range(group):
                    other = images[group * k + i, x, l]
                    for j in range(group):
                        for m, right in enumerate((own[j], second[j])):
                            n = (i * group + j) * 2 + m
                            acc[n] = acc[n] + other * right
            return tuple(acc)

        start = tuple(jnp.zeros((8, nz), jnp.float32) for _ in range(group * group * 2))
        acc = lax.fori_loop(0, nx, plane, start)
        for i in range(group):
            for j in range(group):
                for m in range(2):
                    value = jnp.sum(acc[(i * group + j) * 2 + m])
                    low, high = group * k + i, group * me + j
                    here = jnp.logical_and(trow == low, tcol == high + count * m)
                    there = jnp.logical_and(trow == high, tcol == low + count * m)
                    there = jnp.logical_and(there, k < me)
                    total = jnp.where(jnp.logical_or(here, there), value, total)
        return total

    total = lax.fori_loop(0, me + 1, inner, zero)

    sem = 0
    for name, sums in (("probe", sums_probe), ("sx", sums_sx), ("sy", sums_sy)):
        mine = at[name]
        sums[mine] = total

        def part(shift, sem):
            return pltpu.make_async_remote_copy(
                src_ref=sums.at[mine],
                dst_ref=sums.at[mine],
                send_sem=sum_send.at[sem],
                recv_sem=sum_recv.at[sem],
                device_id={name: lax.rem(mine + shift, size[name])},
                device_id_type=MESH,
            )

        for shift in range(1, size[name]):
            part(shift, sem + shift - 1).start()
        for shift in range(1, size[name]):
            part(shift, sem + shift - 1).wait()
        sem += size[name] - 1
        total = sums[0]
        for other in range(1, size[name]):
            total = total + sums[other]

    full = (8, LANES)
    work = total / cells
    work = jnp.where(tcol == trow + 2 * count, 1.0, work)
    for j in range(count):
        pivot_row = spread(work[j : j + 1, :], full)
        column = spread(work[:, j : j + 1], full)
        pivot = spread(work[j : j + 1, j : j + 1], full)
        work = work - jnp.where(trow > j, column / pivot, 0.0) * pivot_row
    diagonal = jnp.sum(jnp.where(trow == tcol, work, 0.0), axis=1, keepdims=True)
    work = work / spread(jnp.sqrt(diagonal), full)
    inverse = jnp.where(tcol < count, pltpu.roll(work, LANES - 2 * count, 1), 0.0)
    half = jnp.where(tcol < count, pltpu.roll(work, LANES - count, 1), 0.0)
    product = lax.dot_general(
        half,
        inverse,
        (((1,), (1,)), ((), ())),
        precision=lax.Precision.HIGHEST,
        preferred_element_type=jnp.float32,
    )
    projected[...] = product
    inverse_ref[...] = inverse

    def leaving(part, t):
        whole = (slice(None),)
        return pltpu.make_async_copy(
            held(got_probes, whole, part, t), moved(basis, whole, part, t), out_sem.at[part, t]
        )

    for g in range(size["probe"]):

        @pl.when(me == g)
        def _():
            inv = inverse_ref[...]
            factor = [
                [
                    jnp.sum(jnp.where((trow == group * g + r) & (tcol == i), inv, 0.0))
                    for i in range(group * g + r + 1)
                ]
                for r in range(group)
            ]

            def plane(x, carry):
                for l in range(deep):
                    for t in range(wide):
                        part_of = [images[i, x, l, :, tile(t)] for i in range(group * (g + 1))]
                        for r in range(group):
                            out = factor[r][0] * part_of[0]
                            for i in range(1, group * g + r + 1):
                                out = out + factor[r][i] * part_of[i]
                            got_probes[r, x, t, pl.ds(l, 8, stride=deep), :] = out
                return carry

            for part in range(parts):
                lax.fori_loop(part * per, (part + 1) * per, plane, 0)
                for t in range(wide):
                    leaving(part, t).start()

    for part in range(parts):
        for t in range(wide):
            leaving(part, t).wait()


def shards(probes, velocity, diffusivity, obs_weight):
    group, nx, ny, nz = probes.shape
    nprobe, nsx, nsy = (lax.axis_size(name) for name in ("probe", "sx", "sy"))
    count = group * nprobe
    deep = ny // 8
    cells = float(nx * nsx * ny * nsy * nz)
    vmem = pl.BlockSpec(memory_space=pltpu.VMEM)
    f32 = jnp.float32
    total = nprobe + nsx + nsy - 3
    return pl.pallas_call(
        functools.partial(kernel, cells),
        out_shape=(
            jax.ShapeDtypeStruct(probes.shape, f32),
            jax.ShapeDtypeStruct((count, count), f32),
        ),
        in_specs=[pl.BlockSpec(memory_space=pl.ANY)] * 4,
        out_specs=(pl.BlockSpec(memory_space=pl.ANY), vmem),
        scratch_shapes=[
            pltpu.VMEM((group, nx + 2, deep, 8, nz), f32),
            pltpu.VMEM((group, nx + 2, deep, 8, nz), f32),
            pltpu.VMEM((nx + 1, deep, 8, nz), f32),
            pltpu.VMEM((2, 7, nx + 2, deep, 8, nz), f32),
            pltpu.VMEM((2, 2, nx, 1, nz), f32),
            pltpu.VMEM((group, nx, nz // LANES, ny, LANES), f32),
            pltpu.VMEM((3, nx, nz // LANES, ny, LANES), f32),
            pltpu.VMEM((nx, nz // LANES, ny, LANES), f32),
            pltpu.VMEM((nx, nz // LANES, ny, LANES), f32),
            pltpu.VMEM((count, nx, deep, 8, nz), f32),
            pltpu.VMEM((2, 2, group, deep, 8, nz), f32),
            pltpu.VMEM((2, group, nx, 1, nz), f32),
            pltpu.VMEM((2, 2, group, nx, 1, nz), f32),
            pltpu.VMEM((nprobe, 8, LANES), f32),
            pltpu.VMEM((nsx, 8, LANES), f32),
            pltpu.VMEM((nsy, 8, LANES), f32),
            pltpu.VMEM((8, LANES), f32),
            pltpu.SemaphoreType.DMA((2,)),
            pltpu.SemaphoreType.DMA((2, 2)),
            pltpu.SemaphoreType.DMA((2,)),
            pltpu.SemaphoreType.DMA((2, 2)),
            pltpu.SemaphoreType.DMA((2, 2)),
            pltpu.SemaphoreType.DMA((2, 2)),
            pltpu.SemaphoreType.DMA((2, 2 * STEPS)),
            pltpu.SemaphoreType.DMA((nprobe, 2 * STEPS)),
            pltpu.SemaphoreType.DMA((total,)),
            pltpu.SemaphoreType.DMA((total,)),
            pltpu.SemaphoreType.DMA((4, 4, nz // LANES)),
            pltpu.SemaphoreType.DMA((4, nz // LANES)),
        ],
        compiler_params=pltpu.CompilerParams(
            collective_id=0, has_side_effects=True, vmem_limit_bytes=60 * 1024 * 1024
        ),
    )(probes, velocity, diffusivity, obs_weight)


def solution(mesh):
    return jax.shard_map(
        shards,
        mesh=mesh,
        in_specs=(
            P("probe", "sx", "sy", None),
            P(None, "sx", "sy", None),
            P("sx", "sy", None),
            P("sx", "sy", None),
        ),
        out_specs=(P("probe", "sx", "sy", None), P()),
        check_vma=False,
    )
```

```python
import functools

import jax
import jax.numpy as jnp
from jax import lax
from jax.experimental import pallas as pl
from jax.experimental.pallas import tpu as pltpu
from jax.sharding import PartitionSpec as P

STEPS = 4
UNROLL = 1
ROUTES = (0, 1)
MESH = pl.DeviceIdType.MESH
LANES = 128
C0, PX, MX, PY, MY, PZ, MZ = range(7)


def spread(value, shape):
    return jnp.broadcast_to(value, shape)


def kernel(
    cells,
    probes,
    velocity,
    diffusivity,
    weight,
    basis,
    projected,
    field,
    other_field,
    center,
    coef,
    edge,
    got_probes,
    got_velocity,
    got_diffusivity,
    got_weight,
    images,
    passing,
    x_in,
    y_out,
    y_in,
    sums_probe,
    sums_sx,
    sums_sy,
    inverse_ref,
    x_send,
    x_recv,
    y_send,
    y_recv,
    edge_send,
    edge_recv,
    image_send,
    image_recv,
    pass_send,
    pass_recv,
    side_send,
    sum_send,
    sum_recv,
    in_sem,
    out_sem,
):
    group, nx, ny, nz = probes.shape
    deep, wide = ny // 8, nz // LANES
    at = {name: lax.axis_index(name) for name in ("probe", "sx", "sy")}
    size = {name: lax.axis_size(name) for name in ("probe", "sx", "sy")}
    me = at["probe"]
    has = {name: (at[name] > 0, at[name] < size[name] - 1) for name in ("sx", "sy")}

    def tile(t):
        return slice(t * LANES, (t + 1) * LANES)

    parts = 4 if nx % 4 == 0 else 1
    per = nx // parts

    def moved(ref, lead, part, t):
        return ref.at[lead + (pl.ds(part * per, per), slice(None), pl.ds(t * LANES, LANES))]

    def held(ref, lead, part, t):
        return ref.at[lead + (pl.ds(part * per, per), t)]

    arriving = {}
    for part in range(parts):
        for n, (src, dst, lead) in enumerate(
            (
                (diffusivity, got_diffusivity, ()),
                (velocity, got_velocity, (slice(None),)),
                (probes, got_probes, (slice(None),)),
                (weight, got_weight, ()),
            )
        ):
            for t in range(wide):
                copy = pltpu.make_async_copy(
                    moved(src, lead, part, t), held(dst, lead, part, t), in_sem.at[part, n, t]
                )
                arriving[part, n, t] = copy
                copy.start()

    def rows_of(ref, index, l, t):
        return ref[index + (t, pl.ds(l, 8, stride=deep), slice(None))]

    srow = lax.broadcasted_iota(jnp.int32, (8, LANES), 0)
    lane = lax.broadcasted_iota(jnp.int32, (8, LANES), 1)
    zero = jnp.zeros((8, LANES), jnp.float32)

    def shift_z(tiles, up):
        rolled = [pltpu.roll(v, LANES - 1 if up else 1, 1) for v in tiles]
        out = []
        for t in range(wide):
            other = t + 1 if up else t - 1
            if 0 <= other < wide:
                out.append(jnp.where(lane == (LANES - 1 if up else 0), rolled[other], rolled[t]))
            else:
                out.append(rolled[t])
        return out

    def shift_y(tiles, l, up):
        if up:
            return tiles[l + 1] if l + 1 < deep else pltpu.roll(tiles[0], 7, 0)
        return tiles[l - 1] if l > 0 else pltpu.roll(tiles[deep - 1], 1, 0)

    for x in (0, nx + 1):
        for l in range(deep):
            for t in range(wide):
                for ref in (field, other_field):
                    for p in range(group):
                        ref[p, x, l, :, tile(t)] = zero
    for l in range(deep):
        for t in range(wide):
            coef[1, MX, 1, l, :, tile(t)] = zero
            coef[1, PX, nx, l, :, tile(t)] = zero

    barrier = pltpu.get_barrier_semaphore()
    peers = 0
    for name in ("probe", "sx", "sy"):
        for shift in range(1, size[name]):
            peer = lax.rem(at[name] + shift, size[name])
            pl.semaphore_signal(barrier, inc=1, device_id={name: peer}, device_id_type=MESH)
            peers += 1

    across = {
        "probe": lax.rem(me + size["probe"] // 2, size["probe"]),
        "sy": at["sy"] + 1 - 2 * lax.rem(at["sy"], 2),
    }
    pl.semaphore_signal(barrier, inc=1, device_id=across, device_id_type=MESH)
    peers += 1

    def prepare(x, carry):
        last, first = nz - LANES, 0
        plus_y, minus_y = [], []
        for t in range(wide):
            plus_y.append([])
            minus_y.append([])
            for l in range(deep):
                k = rows_of(got_diffusivity, (x,), l, t)
                hx, hy = (0.5 * rows_of(got_velocity, (d, x), l, t) for d in range(2))
                center[x + 1, l, :, tile(t)] = 1.0 - 6.0 * k
                coef[0, PX, x + 1, l, :, tile(t)] = k - hx
                coef[0, MX, x + 1, l, :, tile(t)] = k + hx
                coef[1, MX, x + 2, l, :, tile(t)] = k - hx
                coef[1, PX, x, l, :, tile(t)] = k + hx
                plus_y[t].append(k - hy)
                minus_y[t].append(k + hy)
                for p in range(group):
                    field[p, x + 1, l, :, tile(t)] = rows_of(got_probes, (p, x), l, t)
            edge[0, 0, x, :, tile(t)] = minus_y[t][0][0:1]
            edge[0, 1, x, :, tile(t)] = plus_y[t][deep - 1][7:8]
            for l in range(deep):
                up, down = shift_y(minus_y[t], l, True), shift_y(plus_y[t], l, False)
                plus, minus = plus_y[t][l], minus_y[t][l]
                if l == deep - 1:
                    up, plus = (jnp.where(srow == 7, 0.0, v) for v in (up, plus))
                if l == 0:
                    down, minus = (jnp.where(srow == 0, 0.0, v) for v in (down, minus))
                coef[0, PY, x + 1, l, :, tile(t)] = plus
                coef[0, MY, x + 1, l, :, tile(t)] = minus
                coef[1, PY, x + 1, l, :, tile(t)] = up
                coef[1, MY, x + 1, l, :, tile(t)] = down
        for l in range(deep):
            ks = [rows_of(got_diffusivity, (x,), l, t) for t in range(wide)]
            hs = [0.5 * rows_of(got_velocity, (2, x), l, t) for t in range(wide)]
            plus = [k - h for k, h in zip(ks, hs)]
            minus = [k + h for k, h in zip(ks, hs)]
            up, down = shift_z(minus, True), shift_z(plus, False)
            for v in (plus, up):
                v[wide - 1] = jnp.where(lane == LANES - 1, 0.0, v[wide - 1])
            for v in (minus, down):
                v[0] = jnp.where(lane == 0, 0.0, v[0])
            for t in range(wide):
                coef[0, PZ, x + 1, l, :, tile(t)] = plus[t]
                coef[0, MZ, x + 1, l, :, tile(t)] = minus[t]
                coef[1, PZ, x + 1, l, :, tile(t)] = up[t]
                coef[1, MZ, x + 1, l, :, tile(t)] = down[t]
        return carry

    for part in range(parts):
        for n in range(3):
            for t in range(wide):
                arriving[part, n, t].wait()
        lax.fori_loop(part * per, (part + 1) * per, prepare, 0)

    def fill():
        def one(x, carry):
            for p in range(group):
                for t in range(wide):
                    y_out[0, p, x, :, tile(t)] = field[p, x + 1, 0, 0:1, tile(t)]
                    y_out[1, p, x, :, tile(t)] = field[p, x + 1, deep - 1, 7:8, tile(t)]
            return carry

        lax.fori_loop(0, nx, one, 0)

    fill()
    pl.semaphore_wait(barrier, peers)

    def remote(src, dst, send, recv, name, target):
        return pltpu.make_async_remote_copy(
            src_ref=src,
            dst_ref=dst,
            send_sem=send,
            recv_sem=recv,
            device_id={name: target},
            device_id_type=MESH,
        )

    def edges(name, side, came):
        n = 0 if name == "sx" else 1
        into = side if came else 1 - side
        if name == "sx":
            src = coef.at[0, PX, nx] if side else coef.at[0, MX, 1]
            dst = coef.at[1, PX, nx] if into else coef.at[1, MX, 1]
        else:
            src, dst = edge.at[0, side], edge.at[1, into]
        target = at[name] + (1 if side else -1)
        return remote(src, dst, edge_send.at[n, side], edge_recv.at[n, into], name, target)

    def face(name, side, now, came=False):
        into = side if came else 1 - side
        target = at[name] + (1 if side else -1)
        if name == "sx":
            ref = other_field if now else field
            src, dst = ref.at[:, nx if side else 1], x_in.at[now, into]
            return remote(src, dst, x_send.at[side], x_recv.at[now, into], name, target)
        src, dst = y_out.at[side], y_in.at[now, into]
        return remote(src, dst, y_send.at[side], y_recv.at[now, into], name, target)

    def local(old, new, mode):
        def plane(x, carry):
            for p in range(group):
                u = [[old[p, x, l, :, tile(t)] for t in range(wide)] for l in range(deep)]
                by_tile = [[u[l][t] for l in range(deep)] for t in range(wide)]
                for l in range(deep):
                    up_z, down_z = shift_z(u[l], True), shift_z(u[l], False)
                    for t in range(wide):
                        w = tile(t)
                        r = center[x, l, :, w] * u[l][t]
                        r = r + (
                            coef[mode, PX, x, l, :, w] * old[p, x + 1, l, :, w]
                            + coef[mode, MX, x, l, :, w] * old[p, x - 1, l, :, w]
                        )
                        r = r + (
                            coef[mode, PY, x, l, :, w] * shift_y(by_tile[t], l, True)
                            + coef[mode, MY, x, l, :, w] * shift_y(by_tile[t], l, False)
                        )
                        r = r + (
                            coef[mode, PZ, x, l, :, w] * up_z[t]
                            + coef[mode, MZ, x, l, :, w] * down_z[t]
                        )
                        new[p, x, l, :, w] = r
            return carry

        lax.fori_loop(1, nx + 1, plane, 0, unroll=UNROLL)

    def fix_x(slot, new, side, mode):
        x = nx if side else 1
        for l in range(deep):
            for t in range(wide):
                w = tile(t)
                c = coef[mode, PX if side else MX, x, l, :, w]
                for p in range(group):
                    add = c * x_in[slot, side, p, l, :, w]
                    new[p, x, l, :, w] = new[p, x, l, :, w] + add

    def fix_y(slot, new, side, mode):
        l, row = (deep - 1, 7) if side else (0, 0)

        many = 4 if nx % 4 == 0 else 1

        def some(n, carry):
            found = []
            for k in range(many):
                x = n * many + k
                for t in range(wide):
                    w = tile(t)
                    c = spread(edge[mode, side, x, :, w], (8, LANES))
                    for p in range(group):
                        add = c * spread(y_in[slot, side, p, x, :, w], (8, LANES))
                        v = new[p, x + 1, l, :, w] + jnp.where(srow == row, add, 0.0)
                        found.append((p, x, w, v))
            for p, x, w, v in found:
                new[p, x + 1, l, :, w] = v
                y_out[side, p, x, :, w] = v[row : row + 1]
            return carry

        lax.fori_loop(0, nx // many, some, 0)

    chunks = 2 * STEPS
    thick = nx // chunks if nx >= chunks else nx

    def image_copy(pair, target, sem):
        ref = images.at[pl.ds(group * pair, group)]
        return remote(
            ref, ref, image_send.at[sem, 0], image_recv.at[pair, 0, 0], "probe", target
        )

    def piece(pair, half, chunk):
        return images.at[group * pair + half, pl.ds(chunk * thick, thick)]

    def straight(half, chunk, came=False):
        pair = me - 2 if came else me
        ref = piece(pair, half, chunk)
        recv = image_recv.at[pair, half, chunk]
        return remote(ref, ref, image_send.at[1 + half, chunk], recv, "probe", across["probe"])

    def hop(half, chunk, came=False):
        pair = me - 2 if came else me
        return pltpu.make_async_remote_copy(
            src_ref=piece(pair, half, chunk),
            dst_ref=passing.at[pl.ds(chunk * thick, thick)],
            send_sem=image_send.at[1 + half, chunk],
            recv_sem=pass_recv.at[chunk],
            device_id=across,
            device_id_type=MESH,
        )

    def onward(half, chunk):
        return remote(
            passing.at[pl.ds(chunk * thick, thick)],
            piece(me - 2, half, chunk),
            pass_send.at[chunk],
            image_recv.at[me - 2, half, chunk],
            "sy",
            across["sy"],
        )

    def beside(half, chunk, pair):
        ref = piece(pair, half, chunk)
        send, recv = side_send.at[half, chunk], image_recv.at[pair, half, chunk]
        return remote(ref, ref, send, recv, "probe", 5 - me)

    def dispatch(chunk):
        @pl.when(me < 2)
        def _():
            for half in range(group):
                (hop if ROUTES[half] else straight)(half, chunk).start()

    def pass_on(chunk):
        @pl.when(me >= 2)
        def _():
            for half in range(group):
                if ROUTES[half]:
                    hop(half, chunk, True).wait_recv()
                    onward(half, chunk).start()

    def relay(chunk):
        @pl.when(me >= 2)
        def _():
            for half in range(group):
                straight(half, chunk, True).wait_recv()
                beside(half, chunk, me - 2).start()

    def begin(name, side, now, when=True):
        @pl.when(jnp.logical_and(has[name][side], when))
        def _():
            face(name, side, now).start()

    def begin_all():
        for name in ("sy", "sx"):
            for side in range(2):
                begin(name, side, 0)

    def run(second):
        def step(i, now, mode, send):
            old, new = (other_field, field) if now else (field, other_field)
            if second:
                dispatch(i)

            local(old, new, mode)
            if second:

                @pl.when(i >= 1)
                def _():
                    pass_on(i - 1)

                @pl.when(i >= 3)
                def _():
                    relay(i - 3)

            for name in ("sx", "sy"):
                for side in range(2):

                    @pl.when(has[name][side])
                    def _():
                        face(name, side, now).wait_send()
                        face(name, side, now, True).wait_recv()
                        (fix_x if name == "sx" else fix_y)(now, new, side, mode)

                    if name == "sy":
                        begin(name, side, 1 - now, send)

            for side in range(2):
                begin("sx", side, 1 - now, send)

        def both(i, carry):
            mode = 2 * i // STEPS
            step(2 * i, 0, mode, True)
            step(2 * i + 1, 1, mode, jnp.logical_and(2 * i != STEPS - 2, i != STEPS - 1))

            @pl.when(2 * i == STEPS - 2)
            def _():
                def weigh(x, carry):
                    found = []
                    for l in range(deep):
                        for t in range(wide):
                            w = tile(t)
                            c = rows_of(got_weight, (x,), l, t)
                            for p in range(group):
                                found.append((p, l, w, c * field[p, x + 1, l, :, w]))
                    for p, l, w, v in found:
                        field[p, x + 1, l, :, w] = v
                        if l == 0:
                            y_out[0, p, x, :, w] = v[0:1]
                        if l == deep - 1:
                            y_out[1, p, x, :, w] = v[7:8]
                    return carry

                lax.fori_loop(0, nx, weigh, 0)
                begin_all()
                if not second:
                    for name in ("sx", "sy"):
                        for side in range(2):

                            @pl.when(has[name][side])
                            def _():
                                edges(name, side, False).wait_send()
                                edges(name, side, True).wait_recv()

            return carry

        begin_all()
        lax.fori_loop(0, STEPS, both, 0)

    for name in ("sx", "sy"):
        for side in range(2):

            @pl.when(has[name][side])
            def _():
                edges(name, side, False).start()

    for part in range(parts):
        for t in range(wide):
            arriving[part, 3, t].wait()

    run(False)

    def keep(x, carry):
        for p in range(group):
            images[group * me + p, x] = field[p, x + 1]
        return carry

    lax.fori_loop(0, nx, keep, 0)


    @pl.when(me == 0)
    def _():
        image_copy(0, 1, 0).start()

    @pl.when(me == 2)
    def _():
        image_copy(2, 3, 0).start()

    run(True)

    pass_on(chunks - 1)
    for chunk in range(chunks - 3, chunks):
        relay(chunk)

    @pl.when(me == 0)
    def _():
        image_copy(0, 1, 0).wait_send()

    @pl.when(me == 1)
    def _():
        image_copy(0, 2, 0).wait_recv()

    @pl.when(me == 2)
    def _():
        image_copy(2, 3, 0).wait_send()

    @pl.when(me == 3)
    def _():
        image_copy(2, 2, 0).wait_recv()

    @pl.when(me < 2)
    def _():
        for chunk in range(chunks):
            for half in range(group):
                (hop if ROUTES[half] else straight)(half, chunk).wait_send()

    @pl.when(me >= 2)
    def _():
        for chunk in range(chunks):
            for half in range(group):
                if ROUTES[half]:
                    onward(half, chunk).wait_send()
                beside(half, chunk, me - 2).wait_send()
                beside(half, chunk, 3 - me).wait_recv()

    trow, tcol = srow, lane
    count = size["probe"] * group

    def inner(k, total):
        def plane(x, acc):
            acc = list(acc)
            for l in range(deep):
                own = [images[group * me + j, x, l] for j in range(group)]
                second = [field[j, x + 1, l] for j in range(group)]
                for i in range(group):
                    other = images[group * k + i, x, l]
                    for j in range(group):
                        for m, right in enumerate((own[j], second[j])):
                            n = (i * group + j) * 2 + m
                            acc[n] = acc[n] + other * right
            return tuple(acc)

        start = tuple(jnp.zeros((8, nz), jnp.float32) for _ in range(group * group * 2))
        acc = lax.fori_loop(0, nx, plane, start)
        for i in range(group):
            for j in range(group):
                for m in range(2):
                    value = jnp.sum(acc[(i * group + j) * 2 + m])
                    low, high = group * k + i, group * me + j
                    here = jnp.logical_and(trow == low, tcol == high + count * m)
                    there = jnp.logical_and(trow == high, tcol == low + count * m)
                    there = jnp.logical_and(there, k < me)
                    total = jnp.where(jnp.logical_or(here, there), value, total)
        return total

    total = lax.fori_loop(0, me + 1, inner, zero)

    sem = 0
    for name, sums in (("probe", sums_probe), ("sx", sums_sx), ("sy", sums_sy)):
        mine = at[name]
        sums[mine] = total

        def part(shift, sem):
            return pltpu.make_async_remote_copy(
                src_ref=sums.at[mine],
                dst_ref=sums.at[mine],
                send_sem=sum_send.at[sem],
                recv_sem=sum_recv.at[sem],
                device_id={name: lax.rem(mine + shift, size[name])},
                device_id_type=MESH,
            )

        for shift in range(1, size[name]):
            part(shift, sem + shift - 1).start()
        for shift in range(1, size[name]):
            part(shift, sem + shift - 1).wait()
        sem += size[name] - 1
        total = sums[0]
        for other in range(1, size[name]):
            total = total + sums[other]

    full = (8, LANES)
    work = total / cells
    work = jnp.where(tcol == trow + 2 * count, 1.0, work)
    for j in range(count):
        pivot_row = spread(work[j : j + 1, :], full)
        column = spread(work[:, j : j + 1], full)
        pivot = spread(work[j : j + 1, j : j + 1], full)
        work = work - jnp.where(trow > j, column / pivot, 0.0) * pivot_row
    diagonal = jnp.sum(jnp.where(trow == tcol, work, 0.0), axis=1, keepdims=True)
    work = work / spread(jnp.sqrt(diagonal), full)
    inverse = jnp.where(tcol < count, pltpu.roll(work, LANES - 2 * count, 1), 0.0)
    half = jnp.where(tcol < count, pltpu.roll(work, LANES - count, 1), 0.0)
    product = lax.dot_general(
        half,
        inverse,
        (((1,), (1,)), ((), ())),
        precision=lax.Precision.HIGHEST,
        preferred_element_type=jnp.float32,
    )
    projected[...] = product
    inverse_ref[...] = inverse

    def leaving(part, t):
        whole = (slice(None),)
        return pltpu.make_async_copy(
            held(got_probes, whole, part, t), moved(basis, whole, part, t), out_sem.at[part, t]
        )

    for g in range(size["probe"]):

        @pl.when(me == g)
        def _():
            inv = inverse_ref[...]
            factor = [
                [
                    jnp.sum(jnp.where((trow == group * g + r) & (tcol == i), inv, 0.0))
                    for i in range(group * g + r + 1)
                ]
                for r in range(group)
            ]

            def plane(x, carry):
                for l in range(deep):
                    for t in range(wide):
                        part_of = [images[i, x, l, :, tile(t)] for i in range(group * (g + 1))]
                        for r in range(group):
                            out = factor[r][0] * part_of[0]
                            for i in range(1, group * g + r + 1):
                                out = out + factor[r][i] * part_of[i]
                            got_probes[r, x, t, pl.ds(l, 8, stride=deep), :] = out
                return carry

            for part in range(parts):
                lax.fori_loop(part * per, (part + 1) * per, plane, 0)
                for t in range(wide):
                    leaving(part, t).start()

    for part in range(parts):
        for t in range(wide):
            leaving(part, t).wait()


def shards(probes, velocity, diffusivity, obs_weight):
    group, nx, ny, nz = probes.shape
    nprobe, nsx, nsy = (lax.axis_size(name) for name in ("probe", "sx", "sy"))
    count = group * nprobe
    deep = ny // 8
    cells = float(nx * nsx * ny * nsy * nz)
    vmem = pl.BlockSpec(memory_space=pltpu.VMEM)
    f32 = jnp.float32
    total = nprobe + nsx + nsy - 3
    return pl.pallas_call(
        functools.partial(kernel, cells),
        out_shape=(
            jax.ShapeDtypeStruct(probes.shape, f32),
            jax.ShapeDtypeStruct((count, count), f32),
        ),
        in_specs=[pl.BlockSpec(memory_space=pl.ANY)] * 4,
        out_specs=(pl.BlockSpec(memory_space=pl.ANY), vmem),
        scratch_shapes=[
            pltpu.VMEM((group, nx + 2, deep, 8, nz), f32),
            pltpu.VMEM((group, nx + 2, deep, 8, nz), f32),
            pltpu.VMEM((nx + 1, deep, 8, nz), f32),
            pltpu.VMEM((2, 7, nx + 2, deep, 8, nz), f32),
            pltpu.VMEM((2, 2, nx, 1, nz), f32),
            pltpu.VMEM((group, nx, nz // LANES, ny, LANES), f32),
            pltpu.VMEM((3, nx, nz // LANES, ny, LANES), f32),
            pltpu.VMEM((nx, nz // LANES, ny, LANES), f32),
            pltpu.VMEM((nx, nz // LANES, ny, LANES), f32),
            pltpu.VMEM((count, nx, deep, 8, nz), f32),
            pltpu.VMEM((nx, deep, 8, nz), f32),
            pltpu.VMEM((2, 2, group, deep, 8, nz), f32),
            pltpu.VMEM((2, group, nx, 1, nz), f32),
            pltpu.VMEM((2, 2, group, nx, 1, nz), f32),
            pltpu.VMEM((nprobe, 8, LANES), f32),
            pltpu.VMEM((nsx, 8, LANES), f32),
            pltpu.VMEM((nsy, 8, LANES), f32),
            pltpu.VMEM((8, LANES), f32),
            pltpu.SemaphoreType.DMA((2,)),
            pltpu.SemaphoreType.DMA((2, 2)),
            pltpu.SemaphoreType.DMA((2,)),
            pltpu.SemaphoreType.DMA((2, 2)),
            pltpu.SemaphoreType.DMA((2, 2)),
            pltpu.SemaphoreType.DMA((2, 2)),
            pltpu.SemaphoreType.DMA((1 + group, 2 * STEPS)),
            pltpu.SemaphoreType.DMA((nprobe, group, 2 * STEPS)),
            pltpu.SemaphoreType.DMA((2 * STEPS,)),
            pltpu.SemaphoreType.DMA((2 * STEPS,)),
            pltpu.SemaphoreType.DMA((group, 2 * STEPS)),
            pltpu.SemaphoreType.DMA((total,)),
            pltpu.SemaphoreType.DMA((total,)),
            pltpu.SemaphoreType.DMA((4, 4, nz // LANES)),
            pltpu.SemaphoreType.DMA((4, nz // LANES)),
        ],
        compiler_params=pltpu.CompilerParams(
            collective_id=0, has_side_effects=True, vmem_limit_bytes=60 * 1024 * 1024
        ),
    )(probes, velocity, diffusivity, obs_weight)


def solution(mesh):
    return jax.shard_map(
        shards,
        mesh=mesh,
        in_specs=(
            P("probe", "sx", "sy", None),
            P(None, "sx", "sy", None),
            P("sx", "sy", None),
            P("sx", "sy", None),
        ),
        out_specs=(P("probe", "sx", "sy", None), P()),
        check_vma=False,
    )
```

```python
import functools

import jax
import jax.numpy as jnp
from jax import lax
from jax.experimental import pallas as pl
from jax.experimental.pallas import tpu as pltpu
from jax.sharding import PartitionSpec as P

STEPS = 4
UNROLL = 1
ROUTES = (0, 1)
MANY = 8
BOTH = 2
MESH = pl.DeviceIdType.MESH
LANES = 128
C0, PX, MX, PY, MY, PZ, MZ = range(7)


def spread(value, shape):
    return jnp.broadcast_to(value, shape)


def kernel(
    cells,
    probes,
    velocity,
    diffusivity,
    weight,
    basis,
    projected,
    field,
    other_field,
    center,
    coef,
    edge,
    got_probes,
    got_velocity,
    got_diffusivity,
    got_weight,
    images,
    passing,
    x_in,
    y_out,
    y_in,
    sums_slab,
    sums_line,
    inverse_ref,
    x_send,
    x_recv,
    y_send,
    y_recv,
    edge_send,
    edge_recv,
    image_send,
    image_recv,
    pass_send,
    pass_recv,
    side_send,
    sum_send,
    sum_recv,
    in_sem,
    out_sem,
):
    group, nx, ny, nz = probes.shape
    deep, wide = ny // 8, nz // LANES
    at = {name: lax.axis_index(name) for name in ("probe", "sx", "sy")}
    size = {name: lax.axis_size(name) for name in ("probe", "sx", "sy")}
    me = at["probe"]
    has = {name: (at[name] > 0, at[name] < size[name] - 1) for name in ("sx", "sy")}

    def tile(t):
        return slice(t * LANES, (t + 1) * LANES)

    parts = 4 if nx % 4 == 0 else 1
    per = nx // parts

    def moved(ref, lead, part, t):
        return ref.at[lead + (pl.ds(part * per, per), slice(None), pl.ds(t * LANES, LANES))]

    def held(ref, lead, part, t):
        return ref.at[lead + (pl.ds(part * per, per), t)]

    arriving = {}
    for part in range(parts):
        for n, (src, dst, lead) in enumerate(
            (
                (diffusivity, got_diffusivity, ()),
                (velocity, got_velocity, (slice(None),)),
                (probes, got_probes, (slice(None),)),
                (weight, got_weight, ()),
            )
        ):
            for t in range(wide):
                copy = pltpu.make_async_copy(
                    moved(src, lead, part, t), held(dst, lead, part, t), in_sem.at[part, n, t]
                )
                arriving[part, n, t] = copy
                copy.start()

    def rows_of(ref, index, l, t):
        return ref[index + (t, pl.ds(l, 8, stride=deep), slice(None))]

    srow = lax.broadcasted_iota(jnp.int32, (8, LANES), 0)
    lane = lax.broadcasted_iota(jnp.int32, (8, LANES), 1)
    zero = jnp.zeros((8, LANES), jnp.float32)

    def shift_z(tiles, up):
        rolled = [pltpu.roll(v, LANES - 1 if up else 1, 1) for v in tiles]
        out = []
        for t in range(wide):
            other = t + 1 if up else t - 1
            if 0 <= other < wide:
                out.append(jnp.where(lane == (LANES - 1 if up else 0), rolled[other], rolled[t]))
            else:
                out.append(rolled[t])
        return out

    def shift_y(tiles, l, up):
        if up:
            return tiles[l + 1] if l + 1 < deep else pltpu.roll(tiles[0], 7, 0)
        return tiles[l - 1] if l > 0 else pltpu.roll(tiles[deep - 1], 1, 0)

    for x in (0, nx + 1):
        for l in range(deep):
            for t in range(wide):
                for ref in (field, other_field):
                    for p in range(group):
                        ref[p, x, l, :, tile(t)] = zero
    for l in range(deep):
        for t in range(wide):
            coef[1, MX, 1, l, :, tile(t)] = zero
            coef[1, PX, nx, l, :, tile(t)] = zero

    barrier = pltpu.get_barrier_semaphore()
    peers = 0
    nsx = size["sx"]
    slab, slabs = me * nsx + at["sx"], size["probe"] * nsx

    def in_slab(shift):
        other = lax.rem(slab + shift, slabs)
        return {"probe": other // nsx, "sx": lax.rem(other, nsx)}

    def in_line(shift):
        return {"sy": lax.rem(at["sy"] + shift, size["sy"])}

    stages = ((in_slab, slab, slabs), (in_line, at["sy"], size["sy"]))
    for who, mine, members in stages:
        for shift in range(1, members):
            pl.semaphore_signal(barrier, inc=1, device_id=who(shift), device_id_type=MESH)
            peers += 1

    across = {
        "probe": lax.rem(me + size["probe"] // 2, size["probe"]),
        "sy": at["sy"] + 1 - 2 * lax.rem(at["sy"], 2),
    }
    pl.semaphore_signal(barrier, inc=1, device_id=across, device_id_type=MESH)
    peers += 1

    def prepare(x, carry):
        last, first = nz - LANES, 0
        plus_y, minus_y = [], []
        for t in range(wide):
            plus_y.append([])
            minus_y.append([])
            for l in range(deep):
                k = rows_of(got_diffusivity, (x,), l, t)
                hx, hy = (0.5 * rows_of(got_velocity, (d, x), l, t) for d in range(2))
                center[x + 1, l, :, tile(t)] = 1.0 - 6.0 * k
                coef[0, PX, x + 1, l, :, tile(t)] = k - hx
                coef[0, MX, x + 1, l, :, tile(t)] = k + hx
                coef[1, MX, x + 2, l, :, tile(t)] = k - hx
                coef[1, PX, x, l, :, tile(t)] = k + hx
                plus_y[t].append(k - hy)
                minus_y[t].append(k + hy)
                for p in range(group):
                    field[p, x + 1, l, :, tile(t)] = rows_of(got_probes, (p, x), l, t)
            edge[0, 0, x, :, tile(t)] = minus_y[t][0][0:1]
            edge[0, 1, x, :, tile(t)] = plus_y[t][deep - 1][7:8]
            for l in range(deep):
                up, down = shift_y(minus_y[t], l, True), shift_y(plus_y[t], l, False)
                plus, minus = plus_y[t][l], minus_y[t][l]
                if l == deep - 1:
                    up, plus = (jnp.where(srow == 7, 0.0, v) for v in (up, plus))
                if l == 0:
                    down, minus = (jnp.where(srow == 0, 0.0, v) for v in (down, minus))
                coef[0, PY, x + 1, l, :, tile(t)] = plus
                coef[0, MY, x + 1, l, :, tile(t)] = minus
                coef[1, PY, x + 1, l, :, tile(t)] = up
                coef[1, MY, x + 1, l, :, tile(t)] = down
        for l in range(deep):
            ks = [rows_of(got_diffusivity, (x,), l, t) for t in range(wide)]
            hs = [0.5 * rows_of(got_velocity, (2, x), l, t) for t in range(wide)]
            plus = [k - h for k, h in zip(ks, hs)]
            minus = [k + h for k, h in zip(ks, hs)]
            up, down = shift_z(minus, True), shift_z(plus, False)
            for v in (plus, up):
                v[wide - 1] = jnp.where(lane == LANES - 1, 0.0, v[wide - 1])
            for v in (minus, down):
                v[0] = jnp.where(lane == 0, 0.0, v[0])
            for t in range(wide):
                coef[0, PZ, x + 1, l, :, tile(t)] = plus[t]
                coef[0, MZ, x + 1, l, :, tile(t)] = minus[t]
                coef[1, PZ, x + 1, l, :, tile(t)] = up[t]
                coef[1, MZ, x + 1, l, :, tile(t)] = down[t]
        return carry

    for part in range(parts):
        for n in range(3):
            for t in range(wide):
                arriving[part, n, t].wait()
        lax.fori_loop(part * per, (part + 1) * per, prepare, 0)

    def fill():
        def one(x, carry):
            for p in range(group):
                for t in range(wide):
                    y_out[0, p, x, :, tile(t)] = field[p, x + 1, 0, 0:1, tile(t)]
                    y_out[1, p, x, :, tile(t)] = field[p, x + 1, deep - 1, 7:8, tile(t)]
            return carry

        lax.fori_loop(0, nx, one, 0, unroll=4 if nx % 4 == 0 else 1)

    fill()
    pl.semaphore_wait(barrier, peers)

    def remote(src, dst, send, recv, name, target):
        return pltpu.make_async_remote_copy(
            src_ref=src,
            dst_ref=dst,
            send_sem=send,
            recv_sem=recv,
            device_id={name: target},
            device_id_type=MESH,
        )

    def edges(name, side, came):
        n = 0 if name == "sx" else 1
        into = side if came else 1 - side
        if name == "sx":
            src = coef.at[0, PX, nx] if side else coef.at[0, MX, 1]
            dst = coef.at[1, PX, nx] if into else coef.at[1, MX, 1]
        else:
            src, dst = edge.at[0, side], edge.at[1, into]
        target = at[name] + (1 if side else -1)
        return remote(src, dst, edge_send.at[n, side], edge_recv.at[n, into], name, target)

    def face(name, side, now, came=False):
        into = side if came else 1 - side
        target = at[name] + (1 if side else -1)
        if name == "sx":
            ref = other_field if now else field
            src, dst = ref.at[:, nx if side else 1], x_in.at[now, into]
            return remote(src, dst, x_send.at[side], x_recv.at[now, into], name, target)
        src, dst = y_out.at[side], y_in.at[now, into]
        return remote(src, dst, y_send.at[side], y_recv.at[now, into], name, target)

    def local(old, new, mode):
        def plane(x, carry):
            for p in range(group):
                u = [[old[p, x, l, :, tile(t)] for t in range(wide)] for l in range(deep)]
                by_tile = [[u[l][t] for l in range(deep)] for t in range(wide)]
                for l in range(deep):
                    up_z, down_z = shift_z(u[l], True), shift_z(u[l], False)
                    for t in range(wide):
                        w = tile(t)
                        r = center[x, l, :, w] * u[l][t]
                        r = r + (
                            coef[mode, PX, x, l, :, w] * old[p, x + 1, l, :, w]
                            + coef[mode, MX, x, l, :, w] * old[p, x - 1, l, :, w]
                        )
                        r = r + (
                            coef[mode, PY, x, l, :, w] * shift_y(by_tile[t], l, True)
                            + coef[mode, MY, x, l, :, w] * shift_y(by_tile[t], l, False)
                        )
                        r = r + (
                            coef[mode, PZ, x, l, :, w] * up_z[t]
                            + coef[mode, MZ, x, l, :, w] * down_z[t]
                        )
                        new[p, x, l, :, w] = r
            return carry

        lax.fori_loop(1, nx + 1, plane, 0, unroll=UNROLL)

    def fix_x(slot, new, side, mode):
        x = nx if side else 1
        for l in range(deep):
            for t in range(wide):
                w = tile(t)
                c = coef[mode, PX if side else MX, x, l, :, w]
                for p in range(group):
                    add = c * x_in[slot, side, p, l, :, w]
                    new[p, x, l, :, w] = new[p, x, l, :, w] + add

    def fix_y(slot, new, side, mode):
        l, row = (deep - 1, 7) if side else (0, 0)

        many = MANY if nx % MANY == 0 else 1

        def some(n, carry):
            found = []
            for k in range(many):
                x = n * many + k
                for t in range(wide):
                    w = tile(t)
                    c = spread(edge[mode, side, x, :, w], (8, LANES))
                    for p in range(group):
                        add = c * spread(y_in[slot, side, p, x, :, w], (8, LANES))
                        v = new[p, x + 1, l, :, w] + jnp.where(srow == row, add, 0.0)
                        found.append((p, x, w, v))
            for p, x, w, v in found:
                new[p, x + 1, l, :, w] = v
                y_out[side, p, x, :, w] = v[row : row + 1]
            return carry

        lax.fori_loop(0, nx // many, some, 0)

    chunks = 2 * STEPS
    thick = nx // chunks if nx >= chunks else nx

    def image_copy(pair, target, sem):
        ref = images.at[pl.ds(group * pair, group)]
        return remote(
            ref, ref, image_send.at[sem, 0], image_recv.at[pair, 0, 0], "probe", target
        )

    def piece(pair, half, chunk):
        return images.at[group * pair + half, pl.ds(chunk * thick, thick)]

    def straight(half, chunk, came=False):
        pair = me - 2 if came else me
        ref = piece(pair, half, chunk)
        recv = image_recv.at[pair, half, chunk]
        return remote(ref, ref, image_send.at[1 + half, chunk], recv, "probe", across["probe"])

    def hop(half, chunk, came=False):
        pair = me - 2 if came else me
        return pltpu.make_async_remote_copy(
            src_ref=piece(pair, half, chunk),
            dst_ref=passing.at[pl.ds(chunk * thick, thick)],
            send_sem=image_send.at[1 + half, chunk],
            recv_sem=pass_recv.at[chunk],
            device_id=across,
            device_id_type=MESH,
        )

    def onward(half, chunk):
        return remote(
            passing.at[pl.ds(chunk * thick, thick)],
            piece(me - 2, half, chunk),
            pass_send.at[chunk],
            image_recv.at[me - 2, half, chunk],
            "sy",
            across["sy"],
        )

    def beside(half, chunk, pair):
        ref = piece(pair, half, chunk)
        send, recv = side_send.at[half, chunk], image_recv.at[pair, half, chunk]
        return remote(ref, ref, send, recv, "probe", 5 - me)

    def dispatch(chunk):
        @pl.when(me < 2)
        def _():
            for half in range(group):
                (hop if ROUTES[half] else straight)(half, chunk).start()

    def pass_on(chunk):
        @pl.when(me >= 2)
        def _():
            for half in range(group):
                if ROUTES[half]:
                    hop(half, chunk, True).wait_recv()
                    onward(half, chunk).start()

    def relay(chunk):
        @pl.when(me >= 2)
        def _():
            for half in range(group):
                straight(half, chunk, True).wait_recv()
                beside(half, chunk, me - 2).start()

    def begin(name, side, now, when=True):
        @pl.when(jnp.logical_and(has[name][side], when))
        def _():
            face(name, side, now).start()

    def begin_all():
        for name in ("sy", "sx"):
            for side in range(2):
                begin(name, side, 0)

    def run(second):
        def step(i, now, mode, send):
            old, new = (other_field, field) if now else (field, other_field)
            if second:

                dispatch(i)


            local(old, new, mode)
            def forward_pieces():
                @pl.when(i >= 1)
                def _():
                    pass_on(i - 1)

                @pl.when(i >= 3)
                def _():
                    relay(i - 3)

            if second:
                forward_pieces()

            def receive(name, sides):
                for side in sides:

                    @pl.when(has[name][side])
                    def _():
                        face(name, side, now).wait_send()
                        face(name, side, now, True).wait_recv()
                        (fix_x if name == "sx" else fix_y)(now, new, side, mode)

                    if name == "sy":
                        begin(name, side, 1 - now, send)

            receive("sx", (0, 1))
            receive("sy", (0, 1))
            for side in range(2):
                begin("sx", side, 1 - now, send)

        def both(i, carry):
            mode = 2 * i // STEPS
            step(2 * i, 0, mode, True)
            step(2 * i + 1, 1, mode, jnp.logical_and(2 * i != STEPS - 2, i != STEPS - 1))

            @pl.when(2 * i == STEPS - 2)
            def _():
                pair = BOTH if nx % BOTH == 0 else 1

                def weigh(n, carry):
                    found = []
                    for k in range(pair):
                        x = n * pair + k
                        for l in range(deep):
                            for t in range(wide):
                                w = tile(t)
                                c = rows_of(got_weight, (x,), l, t)
                                for p in range(group):
                                    v = c * field[p, x + 1, l, :, w]
                                    found.append((p, x, l, w, v))
                    for p, x, l, w, v in found:
                        field[p, x + 1, l, :, w] = v
                        if l == 0:
                            y_out[0, p, x, :, w] = v[0:1]
                        if l == deep - 1:
                            y_out[1, p, x, :, w] = v[7:8]
                    return carry

                lax.fori_loop(0, nx // pair, weigh, 0)
                begin_all()
                if not second:
                    for name in ("sx", "sy"):
                        for side in range(2):

                            @pl.when(has[name][side])
                            def _():
                                edges(name, side, False).wait_send()
                                edges(name, side, True).wait_recv()

            return carry

        begin_all()
        lax.fori_loop(0, STEPS, both, 0)

    for name in ("sx", "sy"):
        for side in range(2):

            @pl.when(has[name][side])
            def _():
                edges(name, side, False).start()

    for part in range(parts):
        for t in range(wide):
            arriving[part, 3, t].wait()

    run(False)

    def keep(x, carry):
        for p in range(group):
            images[group * me + p, x] = field[p, x + 1]
        return carry

    lax.fori_loop(0, nx, keep, 0, unroll=2 if nx % 2 == 0 else 1)


    @pl.when(me == 0)
    def _():
        image_copy(0, 1, 0).start()

    @pl.when(me == 2)
    def _():
        image_copy(2, 3, 0).start()

    run(True)

    pass_on(chunks - 1)
    for chunk in range(chunks - 3, chunks):
        relay(chunk)

    @pl.when(me == 0)
    def _():
        image_copy(0, 1, 0).wait_send()

    @pl.when(me == 1)
    def _():
        image_copy(0, 2, 0).wait_recv()

    @pl.when(me == 2)
    def _():
        image_copy(2, 3, 0).wait_send()

    @pl.when(me == 3)
    def _():
        image_copy(2, 2, 0).wait_recv()

    @pl.when(me < 2)
    def _():
        for chunk in range(chunks):
            for half in range(group):
                (hop if ROUTES[half] else straight)(half, chunk).wait_send()

    @pl.when(me >= 2)
    def _():
        for chunk in range(chunks):
            for half in range(group):
                if ROUTES[half]:
                    onward(half, chunk).wait_send()
                beside(half, chunk, me - 2).wait_send()
                beside(half, chunk, 3 - me).wait_recv()

    trow, tcol = srow, lane
    count = size["probe"] * group

    def inner(k, total):
        def plane(x, acc):
            acc = list(acc)
            for l in range(deep):
                own = [images[group * me + j, x, l] for j in range(group)]
                second = [field[j, x + 1, l] for j in range(group)]
                for i in range(group):
                    other = images[group * k + i, x, l]
                    for j in range(group):
                        for m, right in enumerate((own[j], second[j])):
                            n = (i * group + j) * 2 + m
                            acc[n] = acc[n] + other * right
            return tuple(acc)

        start = tuple(jnp.zeros((8, nz), jnp.float32) for _ in range(group * group * 2))
        acc = lax.fori_loop(0, nx, plane, start)
        for i in range(group):
            for j in range(group):
                for m in range(2):
                    value = jnp.sum(acc[(i * group + j) * 2 + m])
                    low, high = group * k + i, group * me + j
                    here = jnp.logical_and(trow == low, tcol == high + count * m)
                    there = jnp.logical_and(trow == high, tcol == low + count * m)
                    there = jnp.logical_and(there, k < me)
                    total = jnp.where(jnp.logical_or(here, there), value, total)
        return total

    total = lax.fori_loop(0, me + 1, inner, zero)

    sem = 0
    for (who, mine, members), sums in zip(stages, (sums_slab, sums_line)):
        sums[mine] = total

        def part(shift):
            return pltpu.make_async_remote_copy(
                src_ref=sums.at[mine],
                dst_ref=sums.at[mine],
                send_sem=sum_send.at[sem + shift - 1],
                recv_sem=sum_recv.at[sem + shift - 1],
                device_id=who(shift),
                device_id_type=MESH,
            )

        for shift in range(1, members):
            part(shift).start()
        for shift in range(1, members):
            part(shift).wait()
        sem += members - 1
        total = sums[0]
        for other in range(1, members):
            total = total + sums[other]

    full = (8, LANES)
    work = total / cells
    work = jnp.where(tcol == trow + 2 * count, 1.0, work)
    for j in range(count):
        pivot_row = spread(work[j : j + 1, :], full)
        column = spread(work[:, j : j + 1], full)
        pivot = spread(work[j : j + 1, j : j + 1], full)
        work = work - jnp.where(trow > j, column / pivot, 0.0) * pivot_row
    diagonal = jnp.sum(jnp.where(trow == tcol, work, 0.0), axis=1, keepdims=True)
    work = work / spread(jnp.sqrt(diagonal), full)
    inverse = jnp.where(tcol < count, pltpu.roll(work, LANES - 2 * count, 1), 0.0)
    half = jnp.where(tcol < count, pltpu.roll(work, LANES - count, 1), 0.0)
    product = lax.dot_general(
        half,
        inverse,
        (((1,), (1,)), ((), ())),
        precision=lax.Precision.HIGHEST,
        preferred_element_type=jnp.float32,
    )
    projected[...] = product
    inverse_ref[...] = inverse

    def leaving(part, t):
        whole = (slice(None),)
        return pltpu.make_async_copy(
            held(got_probes, whole, part, t), moved(basis, whole, part, t), out_sem.at[part, t]
        )

    for g in range(size["probe"]):

        @pl.when(me == g)
        def _():
            inv = inverse_ref[...]
            factor = [
                [
                    jnp.sum(jnp.where((trow == group * g + r) & (tcol == i), inv, 0.0))
                    for i in range(group * g + r + 1)
                ]
                for r in range(group)
            ]

            def plane(x, carry):
                for l in range(deep):
                    for t in range(wide):
                        part_of = [images[i, x, l, :, tile(t)] for i in range(group * (g + 1))]
                        for r in range(group):
                            out = factor[r][0] * part_of[0]
                            for i in range(1, group * g + r + 1):
                                out = out + factor[r][i] * part_of[i]
                            got_probes[r, x, t, pl.ds(l, 8, stride=deep), :] = out
                return carry

            for part in range(parts):
                lax.fori_loop(part * per, (part + 1) * per, plane, 0)
                for t in range(wide):
                    leaving(part, t).start()

    for part in range(parts):
        for t in range(wide):
            leaving(part, t).wait()


def shards(probes, velocity, diffusivity, obs_weight):
    group, nx, ny, nz = probes.shape
    nprobe, nsx, nsy = (lax.axis_size(name) for name in ("probe", "sx", "sy"))
    count = group * nprobe
    deep = ny // 8
    cells = float(nx * nsx * ny * nsy * nz)
    vmem = pl.BlockSpec(memory_space=pltpu.VMEM)
    f32 = jnp.float32
    total = nprobe * nsx + nsy - 2
    return pl.pallas_call(
        functools.partial(kernel, cells),
        out_shape=(
            jax.ShapeDtypeStruct(probes.shape, f32),
            jax.ShapeDtypeStruct((count, count), f32),
        ),
        in_specs=[pl.BlockSpec(memory_space=pl.ANY)] * 4,
        out_specs=(pl.BlockSpec(memory_space=pl.ANY), vmem),
        scratch_shapes=[
            pltpu.VMEM((group, nx + 2, deep, 8, nz), f32),
            pltpu.VMEM((group, nx + 2, deep, 8, nz), f32),
            pltpu.VMEM((nx + 1, deep, 8, nz), f32),
            pltpu.VMEM((2, 7, nx + 2, deep, 8, nz), f32),
            pltpu.VMEM((2, 2, nx, 1, nz), f32),
            pltpu.VMEM((group, nx, nz // LANES, ny, LANES), f32),
            pltpu.VMEM((3, nx, nz // LANES, ny, LANES), f32),
            pltpu.VMEM((nx, nz // LANES, ny, LANES), f32),
            pltpu.VMEM((nx, nz // LANES, ny, LANES), f32),
            pltpu.VMEM((count, nx, deep, 8, nz), f32),
            pltpu.VMEM((nx, deep, 8, nz), f32),
            pltpu.VMEM((2, 2, group, deep, 8, nz), f32),
            pltpu.VMEM((2, group, nx, 1, nz), f32),
            pltpu.VMEM((2, 2, group, nx, 1, nz), f32),
            pltpu.VMEM((nprobe * nsx, 8, LANES), f32),
            pltpu.VMEM((nsy, 8, LANES), f32),
            pltpu.VMEM((8, LANES), f32),
            pltpu.SemaphoreType.DMA((2,)),
            pltpu.SemaphoreType.DMA((2, 2)),
            pltpu.SemaphoreType.DMA((2,)),
            pltpu.SemaphoreType.DMA((2, 2)),
            pltpu.SemaphoreType.DMA((2, 2)),
            pltpu.SemaphoreType.DMA((2, 2)),
            pltpu.SemaphoreType.DMA((1 + group, 2 * STEPS)),
            pltpu.SemaphoreType.DMA((nprobe, group, 2 * STEPS)),
            pltpu.SemaphoreType.DMA((2 * STEPS,)),
            pltpu.SemaphoreType.DMA((2 * STEPS,)),
            pltpu.SemaphoreType.DMA((group, 2 * STEPS)),
            pltpu.SemaphoreType.DMA((total,)),
            pltpu.SemaphoreType.DMA((total,)),
            pltpu.SemaphoreType.DMA((4, 4, nz // LANES)),
            pltpu.SemaphoreType.DMA((4, nz // LANES)),
        ],
        compiler_params=pltpu.CompilerParams(
            collective_id=0, has_side_effects=True, vmem_limit_bytes=60 * 1024 * 1024
        ),
    )(probes, velocity, diffusivity, obs_weight)


def solution(mesh):
    return jax.shard_map(
        shards,
        mesh=mesh,
        in_specs=(
            P("probe", "sx", "sy", None),
            P(None, "sx", "sy", None),
            P("sx", "sy", None),
            P("sx", "sy", None),
        ),
        out_specs=(P("probe", "sx", "sy", None), P()),
        check_vma=False,
    )
```

```python
import functools

import jax
import jax.numpy as jnp
from jax import lax
from jax.experimental import pallas as pl
from jax.experimental.pallas import tpu as pltpu
from jax.sharding import PartitionSpec as P

STEPS = 4
UNROLL = 1
ROUTES = (0, 1)
MANY = 8
BOTH = 2
MESH = pl.DeviceIdType.MESH
LANES = 128
C0, PX, MX, PY, MY, PZ, MZ = range(7)


def spread(value, shape):
    return jnp.broadcast_to(value, shape)


def kernel(
    cells,
    probes,
    velocity,
    diffusivity,
    weight,
    basis,
    projected,
    field,
    other_field,
    center,
    coef,
    edge,
    got_probes,
    got_velocity,
    got_diffusivity,
    got_weight,
    images,
    passing,
    x_in,
    y_out,
    y_in,
    sums_slab,
    sums_line,
    inverse_ref,
    x_send,
    x_recv,
    y_send,
    y_recv,
    edge_send,
    edge_recv,
    image_send,
    image_recv,
    pass_send,
    pass_recv,
    side_send,
    sum_send,
    sum_recv,
    in_sem,
    out_sem,
):
    group, nx, ny, nz = probes.shape
    deep, wide = ny // 8, nz // LANES
    at = {name: lax.axis_index(name) for name in ("probe", "sx", "sy")}
    size = {name: lax.axis_size(name) for name in ("probe", "sx", "sy")}
    me = at["probe"]
    has = {name: (at[name] > 0, at[name] < size[name] - 1) for name in ("sx", "sy")}

    def tile(t):
        return slice(t * LANES, (t + 1) * LANES)

    parts = 4 if nx % 4 == 0 else 1
    per = nx // parts

    def moved(ref, lead, part, t):
        return ref.at[lead + (pl.ds(part * per, per), slice(None), pl.ds(t * LANES, LANES))]

    def held(ref, lead, part, t):
        return ref.at[lead + (pl.ds(part * per, per), t)]

    arriving = {}
    for part in range(parts):
        for n, (src, dst, lead) in enumerate(
            (
                (diffusivity, got_diffusivity, ()),
                (velocity, got_velocity, (slice(None),)),
                (probes, got_probes, (slice(None),)),
                (weight, got_weight, ()),
            )
        ):
            for t in range(wide):
                copy = pltpu.make_async_copy(
                    moved(src, lead, part, t), held(dst, lead, part, t), in_sem.at[part, n, t]
                )
                arriving[part, n, t] = copy
                copy.start()

    def rows_of(ref, index, l, t):
        return ref[index + (t, pl.ds(l, 8, stride=deep), slice(None))]

    srow = lax.broadcasted_iota(jnp.int32, (8, LANES), 0)
    lane = lax.broadcasted_iota(jnp.int32, (8, LANES), 1)
    zero = jnp.zeros((8, LANES), jnp.float32)

    def shift_z(tiles, up):
        rolled = [pltpu.roll(v, LANES - 1 if up else 1, 1) for v in tiles]
        out = []
        for t in range(wide):
            other = t + 1 if up else t - 1
            if 0 <= other < wide:
                out.append(jnp.where(lane == (LANES - 1 if up else 0), rolled[other], rolled[t]))
            else:
                out.append(rolled[t])
        return out

    def shift_y(tiles, l, up):
        if up:
            return tiles[l + 1] if l + 1 < deep else pltpu.roll(tiles[0], 7, 0)
        return tiles[l - 1] if l > 0 else pltpu.roll(tiles[deep - 1], 1, 0)

    for x in (0, nx + 1):
        for l in range(deep):
            for t in range(wide):
                for ref in (field, other_field):
                    for p in range(group):
                        ref[p, x, l, :, tile(t)] = zero
    for l in range(deep):
        for t in range(wide):
            coef[1, MX, 1, l, :, tile(t)] = zero
            coef[1, PX, nx, l, :, tile(t)] = zero

    barrier = pltpu.get_barrier_semaphore()
    peers = 0
    nsx = size["sx"]
    slab, slabs = me * nsx + at["sx"], size["probe"] * nsx

    def in_slab(shift):
        other = lax.rem(slab + shift, slabs)
        return {"probe": other // nsx, "sx": lax.rem(other, nsx)}

    def in_line(shift):
        return {"sy": lax.rem(at["sy"] + shift, size["sy"])}

    stages = ((in_slab, slab, slabs), (in_line, at["sy"], size["sy"]))
    for who, mine, members in stages:
        for shift in range(1, members):
            pl.semaphore_signal(barrier, inc=1, device_id=who(shift), device_id_type=MESH)
            peers += 1

    across = {
        "probe": lax.rem(me + size["probe"] // 2, size["probe"]),
        "sy": at["sy"] + 1 - 2 * lax.rem(at["sy"], 2),
    }
    pl.semaphore_signal(barrier, inc=1, device_id=across, device_id_type=MESH)
    peers += 1

    def prepare(x, carry):
        last, first = nz - LANES, 0
        plus_y, minus_y = [], []
        for t in range(wide):
            plus_y.append([])
            minus_y.append([])
            for l in range(deep):
                k = rows_of(got_diffusivity, (x,), l, t)
                hx, hy = (0.5 * rows_of(got_velocity, (d, x), l, t) for d in range(2))
                center[x + 1, l, :, tile(t)] = 1.0 - 6.0 * k
                coef[0, PX, x + 1, l, :, tile(t)] = k - hx
                coef[0, MX, x + 1, l, :, tile(t)] = k + hx
                coef[1, MX, x + 2, l, :, tile(t)] = k - hx
                coef[1, PX, x, l, :, tile(t)] = k + hx
                plus_y[t].append(k - hy)
                minus_y[t].append(k + hy)
                for p in range(group):
                    field[p, x + 1, l, :, tile(t)] = rows_of(got_probes, (p, x), l, t)
            edge[0, 0, x, :, tile(t)] = minus_y[t][0][0:1]
            edge[0, 1, x, :, tile(t)] = plus_y[t][deep - 1][7:8]
            for l in range(deep):
                up, down = shift_y(minus_y[t], l, True), shift_y(plus_y[t], l, False)
                plus, minus = plus_y[t][l], minus_y[t][l]
                if l == deep - 1:
                    up, plus = (jnp.where(srow == 7, 0.0, v) for v in (up, plus))
                if l == 0:
                    down, minus = (jnp.where(srow == 0, 0.0, v) for v in (down, minus))
                coef[0, PY, x + 1, l, :, tile(t)] = plus
                coef[0, MY, x + 1, l, :, tile(t)] = minus
                coef[1, PY, x + 1, l, :, tile(t)] = up
                coef[1, MY, x + 1, l, :, tile(t)] = down
        for l in range(deep):
            ks = [rows_of(got_diffusivity, (x,), l, t) for t in range(wide)]
            hs = [0.5 * rows_of(got_velocity, (2, x), l, t) for t in range(wide)]
            plus = [k - h for k, h in zip(ks, hs)]
            minus = [k + h for k, h in zip(ks, hs)]
            up, down = shift_z(minus, True), shift_z(plus, False)
            for v in (plus, up):
                v[wide - 1] = jnp.where(lane == LANES - 1, 0.0, v[wide - 1])
            for v in (minus, down):
                v[0] = jnp.where(lane == 0, 0.0, v[0])
            for t in range(wide):
                coef[0, PZ, x + 1, l, :, tile(t)] = plus[t]
                coef[0, MZ, x + 1, l, :, tile(t)] = minus[t]
                coef[1, PZ, x + 1, l, :, tile(t)] = up[t]
                coef[1, MZ, x + 1, l, :, tile(t)] = down[t]
        return carry

    for part in range(parts):
        for n in range(3):
            for t in range(wide):
                arriving[part, n, t].wait()
        lax.fori_loop(part * per, (part + 1) * per, prepare, 0)

    def fill():
        def one(x, carry):
            for p in range(group):
                for t in range(wide):
                    y_out[0, p, x, :, tile(t)] = field[p, x + 1, 0, 0:1, tile(t)]
                    y_out[1, p, x, :, tile(t)] = field[p, x + 1, deep - 1, 7:8, tile(t)]
            return carry

        lax.fori_loop(0, nx, one, 0, unroll=4 if nx % 4 == 0 else 1)

    fill()
    pl.semaphore_wait(barrier, peers)

    def remote(src, dst, send, recv, name, target):
        return pltpu.make_async_remote_copy(
            src_ref=src,
            dst_ref=dst,
            send_sem=send,
            recv_sem=recv,
            device_id={name: target},
            device_id_type=MESH,
        )

    def edges(name, side, came):
        n = 0 if name == "sx" else 1
        into = side if came else 1 - side
        if name == "sx":
            src = coef.at[0, PX, nx] if side else coef.at[0, MX, 1]
            dst = coef.at[1, PX, nx] if into else coef.at[1, MX, 1]
        else:
            src, dst = edge.at[0, side], edge.at[1, into]
        target = at[name] + (1 if side else -1)
        return remote(src, dst, edge_send.at[n, side], edge_recv.at[n, into], name, target)

    def face(name, side, now, came=False):
        into = side if came else 1 - side
        target = at[name] + (1 if side else -1)
        if name == "sx":
            ref = other_field if now else field
            src, dst = ref.at[:, nx if side else 1], x_in.at[now, into]
            return remote(src, dst, x_send.at[side], x_recv.at[now, into], name, target)
        src, dst = y_out.at[side], y_in.at[now, into]
        return remote(src, dst, y_send.at[side], y_recv.at[now, into], name, target)

    def local(old, new, mode):
        def plane(x, carry):
            for p in range(group):
                u = [[old[p, x, l, :, tile(t)] for t in range(wide)] for l in range(deep)]
                by_tile = [[u[l][t] for l in range(deep)] for t in range(wide)]
                for l in range(deep):
                    up_z, down_z = shift_z(u[l], True), shift_z(u[l], False)
                    for t in range(wide):
                        w = tile(t)
                        r = center[x, l, :, w] * u[l][t]
                        r = r + (
                            coef[mode, PX, x, l, :, w] * old[p, x + 1, l, :, w]
                            + coef[mode, MX, x, l, :, w] * old[p, x - 1, l, :, w]
                        )
                        r = r + (
                            coef[mode, PY, x, l, :, w] * shift_y(by_tile[t], l, True)
                            + coef[mode, MY, x, l, :, w] * shift_y(by_tile[t], l, False)
                        )
                        r = r + (
                            coef[mode, PZ, x, l, :, w] * up_z[t]
                            + coef[mode, MZ, x, l, :, w] * down_z[t]
                        )
                        new[p, x, l, :, w] = r
            return carry

        lax.fori_loop(1, nx + 1, plane, 0, unroll=UNROLL)

    def fix_x(slot, new, side, mode):
        x = nx if side else 1
        for l in range(deep):
            for t in range(wide):
                w = tile(t)
                c = coef[mode, PX if side else MX, x, l, :, w]
                for p in range(group):
                    add = c * x_in[slot, side, p, l, :, w]
                    new[p, x, l, :, w] = new[p, x, l, :, w] + add

    def fix_y(slot, new, side, mode):
        l, row = (deep - 1, 7) if side else (0, 0)

        many = MANY if nx % MANY == 0 else 1

        def some(n, carry):
            found = []
            for k in range(many):
                x = n * many + k
                for t in range(wide):
                    w = tile(t)
                    c = spread(edge[mode, side, x, :, w], (8, LANES))
                    for p in range(group):
                        add = c * spread(y_in[slot, side, p, x, :, w], (8, LANES))
                        v = new[p, x + 1, l, :, w] + jnp.where(srow == row, add, 0.0)
                        found.append((p, x, w, v))
            for p, x, w, v in found:
                new[p, x + 1, l, :, w] = v
                y_out[side, p, x, :, w] = v[row : row + 1]
            return carry

        lax.fori_loop(0, nx // many, some, 0)

    chunks = 2 * STEPS
    thick = nx // chunks if nx >= chunks else nx

    def image_copy(pair, target, sem):
        ref = images.at[pl.ds(group * pair, group)]
        return remote(
            ref, ref, image_send.at[sem, 0], image_recv.at[pair, 0, 0], "probe", target
        )

    def piece(pair, half, chunk):
        return images.at[group * pair + half, pl.ds(chunk * thick, thick)]

    def straight(half, chunk, came=False):
        pair = me - 2 if came else me
        ref = piece(pair, half, chunk)
        recv = image_recv.at[pair, half, chunk]
        return remote(ref, ref, image_send.at[1 + half, chunk], recv, "probe", across["probe"])

    def hop(half, chunk, came=False):
        pair = me - 2 if came else me
        return pltpu.make_async_remote_copy(
            src_ref=piece(pair, half, chunk),
            dst_ref=passing.at[pl.ds(chunk * thick, thick)],
            send_sem=image_send.at[1 + half, chunk],
            recv_sem=pass_recv.at[chunk],
            device_id=across,
            device_id_type=MESH,
        )

    def onward(half, chunk):
        return remote(
            passing.at[pl.ds(chunk * thick, thick)],
            piece(me - 2, half, chunk),
            pass_send.at[chunk],
            image_recv.at[me - 2, half, chunk],
            "sy",
            across["sy"],
        )

    def beside(half, chunk, pair):
        ref = piece(pair, half, chunk)
        send, recv = side_send.at[half, chunk], image_recv.at[pair, half, chunk]
        return remote(ref, ref, send, recv, "probe", 5 - me)

    def dispatch(chunk):
        @pl.when(me < 2)
        def _():
            for half in range(group):
                (hop if ROUTES[half] else straight)(half, chunk).start()

    def pass_on(chunk):
        @pl.when(me >= 2)
        def _():
            for half in range(group):
                if ROUTES[half]:
                    hop(half, chunk, True).wait_recv()
                    onward(half, chunk).start()

    def relay(chunk):
        @pl.when(me >= 2)
        def _():
            for half in range(group):
                straight(half, chunk, True).wait_recv()
                beside(half, chunk, me - 2).start()

    def begin(name, side, now, when=True):
        @pl.when(jnp.logical_and(has[name][side], when))
        def _():
            face(name, side, now).start()

    def begin_all():
        for name in ("sy", "sx"):
            for side in range(2):
                begin(name, side, 0)

    def run(second):
        def step(i, now, mode, send):
            old, new = (other_field, field) if now else (field, other_field)
            if second:

                dispatch(i)


            local(old, new, mode)
            def forward_pieces():
                @pl.when(i >= 1)
                def _():
                    pass_on(i - 1)

                @pl.when(i >= 3)
                def _():
                    relay(i - 3)

            if second:
                forward_pieces()

            def receive(name, sides):
                for side in sides:

                    @pl.when(has[name][side])
                    def _():
                        face(name, side, now).wait_send()
                        face(name, side, now, True).wait_recv()
                        (fix_x if name == "sx" else fix_y)(now, new, side, mode)

                    if name == "sy":
                        begin(name, side, 1 - now, send)

            receive("sx", (0, 1))
            receive("sy", (0, 1))
            for side in range(2):
                begin("sx", side, 1 - now, send)

        def both(i, carry):
            mode = 2 * i // STEPS
            step(2 * i, 0, mode, True)
            step(2 * i + 1, 1, mode, jnp.logical_and(2 * i != STEPS - 2, i != STEPS - 1))

            @pl.when(2 * i == STEPS - 2)
            def _():
                pair = BOTH if nx % BOTH == 0 else 1

                def weigh(n, carry):
                    found = []
                    for k in range(pair):
                        x = n * pair + k
                        for l in range(deep):
                            for t in range(wide):
                                w = tile(t)
                                c = rows_of(got_weight, (x,), l, t)
                                for p in range(group):
                                    v = c * field[p, x + 1, l, :, w]
                                    found.append((p, x, l, w, v))
                    for p, x, l, w, v in found:
                        field[p, x + 1, l, :, w] = v
                        if l == 0:
                            y_out[0, p, x, :, w] = v[0:1]
                        if l == deep - 1:
                            y_out[1, p, x, :, w] = v[7:8]
                    return carry

                lax.fori_loop(0, nx // pair, weigh, 0)
                begin_all()
                if not second:
                    for name in ("sx", "sy"):
                        for side in range(2):

                            @pl.when(has[name][side])
                            def _():
                                edges(name, side, False).wait_send()
                                edges(name, side, True).wait_recv()

            return carry

        begin_all()
        lax.fori_loop(0, STEPS, both, 0)

    for name in ("sx", "sy"):
        for side in range(2):

            @pl.when(has[name][side])
            def _():
                edges(name, side, False).start()

    for part in range(parts):
        for t in range(wide):
            arriving[part, 3, t].wait()

    run(False)

    def keep(x, carry):
        for p in range(group):
            images[group * me + p, x] = field[p, x + 1]
        return carry

    lax.fori_loop(0, nx, keep, 0, unroll=2 if nx % 2 == 0 else 1)


    @pl.when(me == 0)
    def _():
        image_copy(0, 1, 0).start()

    @pl.when(me == 2)
    def _():
        image_copy(2, 3, 0).start()

    run(True)

    pass_on(chunks - 1)
    for chunk in range(chunks - 3, chunks):
        relay(chunk)

    @pl.when(me == 0)
    def _():
        image_copy(0, 1, 0).wait_send()

    @pl.when(me == 1)
    def _():
        image_copy(0, 2, 0).wait_recv()

    @pl.when(me == 2)
    def _():
        image_copy(2, 3, 0).wait_send()

    @pl.when(me == 3)
    def _():
        image_copy(2, 2, 0).wait_recv()

    @pl.when(me < 2)
    def _():
        for chunk in range(chunks):
            for half in range(group):
                (hop if ROUTES[half] else straight)(half, chunk).wait_send()

    @pl.when(me >= 2)
    def _():
        for chunk in range(chunks):
            for half in range(group):
                if ROUTES[half]:
                    onward(half, chunk).wait_send()
                beside(half, chunk, me - 2).wait_send()
                beside(half, chunk, 3 - me).wait_recv()

    trow, tcol = srow, lane
    count = size["probe"] * group

    def inner(k, total):
        def plane(x, acc):
            acc = list(acc)
            for l in range(deep):
                own = [images[group * me + j, x, l] for j in range(group)]
                second = [field[j, x + 1, l] for j in range(group)]
                for i in range(group):
                    other = images[group * k + i, x, l]
                    for j in range(group):
                        for m, right in enumerate((own[j], second[j])):
                            n = (i * group + j) * 2 + m
                            acc[n] = acc[n] + other * right
            return tuple(acc)

        start = tuple(jnp.zeros((8, nz), jnp.float32) for _ in range(group * group * 2))
        acc = lax.fori_loop(0, nx, plane, start, unroll=4 if nx % 4 == 0 else 1)
        for i in range(group):
            for j in range(group):
                for m in range(2):
                    value = jnp.sum(acc[(i * group + j) * 2 + m])
                    low, high = group * k + i, group * me + j
                    here = jnp.logical_and(trow == low, tcol == high + count * m)
                    there = jnp.logical_and(trow == high, tcol == low + count * m)
                    there = jnp.logical_and(there, k < me)
                    total = jnp.where(jnp.logical_or(here, there), value, total)
        return total

    total = lax.fori_loop(0, me + 1, inner, zero)

    sem = 0
    for (who, mine, members), sums in zip(stages, (sums_slab, sums_line)):
        sums[mine] = total

        def part(shift):
            return pltpu.make_async_remote_copy(
                src_ref=sums.at[mine],
                dst_ref=sums.at[mine],
                send_sem=sum_send.at[sem + shift - 1],
                recv_sem=sum_recv.at[sem + shift - 1],
                device_id=who(shift),
                device_id_type=MESH,
            )

        for shift in range(1, members):
            part(shift).start()
        for shift in range(1, members):
            part(shift).wait()
        sem += members - 1
        total = sums[0]
        for other in range(1, members):
            total = total + sums[other]

    full = (8, LANES)
    work = total / cells
    work = jnp.where(tcol == trow + 2 * count, 1.0, work)
    for j in range(count):
        pivot_row = spread(work[j : j + 1, :], full)
        column = spread(work[:, j : j + 1], full)
        pivot = spread(work[j : j + 1, j : j + 1], full)
        work = work - jnp.where(trow > j, column / pivot, 0.0) * pivot_row
    diagonal = jnp.sum(jnp.where(trow == tcol, work, 0.0), axis=1, keepdims=True)
    work = work / spread(jnp.sqrt(diagonal), full)
    inverse = jnp.where(tcol < count, pltpu.roll(work, LANES - 2 * count, 1), 0.0)
    half = jnp.where(tcol < count, pltpu.roll(work, LANES - count, 1), 0.0)
    product = lax.dot_general(
        half,
        inverse,
        (((1,), (1,)), ((), ())),
        precision=lax.Precision.HIGHEST,
        preferred_element_type=jnp.float32,
    )
    projected[...] = product
    inverse_ref[...] = inverse

    def leaving(part, t):
        whole = (slice(None),)
        return pltpu.make_async_copy(
            held(got_probes, whole, part, t), moved(basis, whole, part, t), out_sem.at[part, t]
        )

    for g in range(size["probe"]):

        @pl.when(me == g)
        def _():
            inv = inverse_ref[...]
            factor = [
                [
                    jnp.sum(jnp.where((trow == group * g + r) & (tcol == i), inv, 0.0))
                    for i in range(group * g + r + 1)
                ]
                for r in range(group)
            ]

            def plane(x, carry):
                for l in range(deep):
                    for t in range(wide):
                        part_of = [images[i, x, l, :, tile(t)] for i in range(group * (g + 1))]
                        for r in range(group):
                            out = factor[r][0] * part_of[0]
                            for i in range(1, group * g + r + 1):
                                out = out + factor[r][i] * part_of[i]
                            got_probes[r, x, t, pl.ds(l, 8, stride=deep), :] = out
                return carry

            for part in range(parts):
                lax.fori_loop(part * per, (part + 1) * per, plane, 0)
                for t in range(wide):
                    leaving(part, t).start()

    for part in range(parts):
        for t in range(wide):
            leaving(part, t).wait()


def shards(probes, velocity, diffusivity, obs_weight):
    group, nx, ny, nz = probes.shape
    nprobe, nsx, nsy = (lax.axis_size(name) for name in ("probe", "sx", "sy"))
    count = group * nprobe
    deep = ny // 8
    cells = float(nx * nsx * ny * nsy * nz)
    vmem = pl.BlockSpec(memory_space=pltpu.VMEM)
    f32 = jnp.float32
    total = nprobe * nsx + nsy - 2
    return pl.pallas_call(
        functools.partial(kernel, cells),
        out_shape=(
            jax.ShapeDtypeStruct(probes.shape, f32),
            jax.ShapeDtypeStruct((count, count), f32),
        ),
        in_specs=[pl.BlockSpec(memory_space=pl.ANY)] * 4,
        out_specs=(pl.BlockSpec(memory_space=pl.ANY), vmem),
        scratch_shapes=[
            pltpu.VMEM((group, nx + 2, deep, 8, nz), f32),
            pltpu.VMEM((group, nx + 2, deep, 8, nz), f32),
            pltpu.VMEM((nx + 1, deep, 8, nz), f32),
            pltpu.VMEM((2, 7, nx + 2, deep, 8, nz), f32),
            pltpu.VMEM((2, 2, nx, 1, nz), f32),
            pltpu.VMEM((group, nx, nz // LANES, ny, LANES), f32),
            pltpu.VMEM((3, nx, nz // LANES, ny, LANES), f32),
            pltpu.VMEM((nx, nz // LANES, ny, LANES), f32),
            pltpu.VMEM((nx, nz // LANES, ny, LANES), f32),
            pltpu.VMEM((count, nx, deep, 8, nz), f32),
            pltpu.VMEM((nx, deep, 8, nz), f32),
            pltpu.VMEM((2, 2, group, deep, 8, nz), f32),
            pltpu.VMEM((2, group, nx, 1, nz), f32),
            pltpu.VMEM((2, 2, group, nx, 1, nz), f32),
            pltpu.VMEM((nprobe * nsx, 8, LANES), f32),
            pltpu.VMEM((nsy, 8, LANES), f32),
            pltpu.VMEM((8, LANES), f32),
            pltpu.SemaphoreType.DMA((2,)),
            pltpu.SemaphoreType.DMA((2, 2)),
            pltpu.SemaphoreType.DMA((2,)),
            pltpu.SemaphoreType.DMA((2, 2)),
            pltpu.SemaphoreType.DMA((2, 2)),
            pltpu.SemaphoreType.DMA((2, 2)),
            pltpu.SemaphoreType.DMA((1 + group, 2 * STEPS)),
            pltpu.SemaphoreType.DMA((nprobe, group, 2 * STEPS)),
            pltpu.SemaphoreType.DMA((2 * STEPS,)),
            pltpu.SemaphoreType.DMA((2 * STEPS,)),
            pltpu.SemaphoreType.DMA((group, 2 * STEPS)),
            pltpu.SemaphoreType.DMA((total,)),
            pltpu.SemaphoreType.DMA((total,)),
            pltpu.SemaphoreType.DMA((4, 4, nz // LANES)),
            pltpu.SemaphoreType.DMA((4, nz // LANES)),
        ],
        compiler_params=pltpu.CompilerParams(
            collective_id=0, has_side_effects=True, vmem_limit_bytes=60 * 1024 * 1024
        ),
    )(probes, velocity, diffusivity, obs_weight)


def solution(mesh):
    return jax.shard_map(
        shards,
        mesh=mesh,
        in_specs=(
            P("probe", "sx", "sy", None),
            P(None, "sx", "sy", None),
            P("sx", "sy", None),
            P("sx", "sy", None),
        ),
        out_specs=(P("probe", "sx", "sy", None), P()),
        check_vma=False,
    )
```
